32 devices in a mesh: clips: 2 (over x), seq: 8 (over z, y), head: 2 (over core).
Axes of the slice: x: 2, y: 2, z: 4, core: 2. Of those that a mesh axis runs over, the one named last changes fastest.
Arguments:
- video_q: bfloat16 [2048, 2048], P(('clips', 'seq'), 'head'), parts along dimension 0, may hold values from -105 to 105
- video_k: bfloat16 [2048, 2048], P(('clips', 'seq'), 'head'), parts along dimension 0, may hold values from -5 to 5
- video_v: bfloat16 [2048, 2048], P(('clips', 'seq'), 'head'), parts along dimension 0, may hold values from -6 to 6
- audio_q: bfloat16 [512, 2048], P(('clips', 'seq'), 'head'), parts along dimension 0, may hold values from -105 to 105
- audio_k: bfloat16 [512, 2048], P(('clips', 'seq'), 'head'), parts along dimension 0, may hold values from -5 to 5
- audio_v: bfloat16 [512, 2048], P(('clips', 'seq'), 'head'), parts along dimension 0, may hold values from -6 to 6
- video_query_gain: float32 [2048], P('head'), may hold values from 1 to 2
- video_key_gain: float32 [2048], P('head'), may hold values from 1 to 2
- audio_query_gain: float32 [2048], P('head'), may hold values from 1 to 2
- audio_key_gain: float32 [2048], P('head'), may hold values from 1 to 2
Outputs:
- video_mixed: bfloat16 [2048, 2048], P(('clips', 'seq'), 'head'), parts along dimension 0
- audio_mixed: bfloat16 [512, 2048], P(('clips', 'seq'), 'head'), parts along dimension 0
The draws below stay inside these ranges and needn't reach their ends.
There are 2 independent parts, one for each index of `clips`. The reference program is written for one: setup_inputs(seed, part) draws one part's arguments, and reference() takes and returns one part's arrays. A program takes and returns all parts, laid end to end along the dimension named above; an argument that names none is the same for every part. Nothing has to cross between parts.
All inputs are finite; a program needn't handle non-finite values.
Results may differ from the reference program's by a relative error of at most 0.02.
Values may be sent and summed in bfloat16 or wider, within the bound.
A program may use at most 128 MiB of HBM per device.

```python
import math
import jax
import jax.numpy as jnp
from jax import lax

HEAD_DIM = 128
VIDEO_HEADS = 16
AUDIO_HEADS = 16
VTOKENS = 1024
ATOKENS = 256


def aligned_pair(key, row_count, col_count):
    queries = jnp.clip(jax.random.normal(jax.random.fold_in(key, 31), (row_count, col_count), jnp.float32), -4.0, 4.0) * 1.25
    key_rows = jnp.clip(jax.random.normal(jax.random.fold_in(key, 37), (row_count, col_count), jnp.float32), -4.0, 4.0) * 1.25
    key_rows = key_rows.at[0, 0].set(5.0)
    key_rows = key_rows.at[1, 1].set(-5.0)
    return (queries, key_rows)


def draw_video_q(key, part):
    return aligned_pair(key, VTOKENS, VIDEO_HEADS * HEAD_DIM)[0].astype(jnp.bfloat16)


def draw_video_k(key, part):
    return aligned_pair(key, VTOKENS, VIDEO_HEADS * HEAD_DIM)[1].astype(jnp.bfloat16)


def draw_audio_q(key, part):
    return aligned_pair(key, ATOKENS, AUDIO_HEADS * HEAD_DIM)[0].astype(jnp.bfloat16)


def draw_audio_k(key, part):
    return aligned_pair(key, ATOKENS, AUDIO_HEADS * HEAD_DIM)[1].astype(jnp.bfloat16)


def steps_of(key, shape, pieces, low, high):
    loudness, own = 1.0, jax.random.fold_in(key, 6)
    for dim, parts in pieces:
        heights = jnp.exp(jax.random.uniform(jax.random.fold_in(own, dim), (parts,), jnp.float32, low / len(pieces), high / len(pieces)))
        loudness = loudness * jnp.repeat(heights, shape[dim] // parts).reshape([-1 if axis == dim else 1 for axis in range(len(shape))])
    return loudness


def bell_draw(key, extent, deviation, most, cuts=(), kind=jnp.bfloat16):
    array = jax.random.normal(key, extent, jnp.float32) * deviation
    if len(cuts) > 0:
        array = steps_of(key, extent, cuts, -0.22, 0.18) * array
    return jnp.clip(array, min=-most, max=most).astype(kind)


def setup_inputs(seed: int = 0, part: int = 0) -> dict:
    seeds = jax.random.split(jax.random.key(seed), 11)
    own_keys = jax.random.split(jax.random.fold_in(seeds[10], part), 11)
    video_q = draw_video_q(jax.random.fold_in(jax.random.fold_in(seeds[10], part), 71), part)
    video_k = draw_video_k(jax.random.fold_in(jax.random.fold_in(seeds[10], part), 71), part)
    video_v = bell_draw(own_keys[2], (VTOKENS, VIDEO_HEADS * HEAD_DIM), 1.0, 6.0, ((0, 8), (1, 2)))
    audio_q = draw_audio_q(jax.random.fold_in(jax.random.fold_in(seeds[10], part), 71), part)
    audio_k = draw_audio_k(jax.random.fold_in(jax.random.fold_in(seeds[10], part), 71), part)
    audio_v = bell_draw(own_keys[5], (ATOKENS, AUDIO_HEADS * HEAD_DIM), 1.0, 6.0, ((0, 8), (1, 2)))
    video_query_gain = jnp.clip(jnp.exp(math.log(2.0) - 0.6931472 * jax.random.uniform(seeds[6], (VIDEO_HEADS * HEAD_DIM,), jnp.float32) ** steps_of(seeds[6], (VIDEO_HEADS * HEAD_DIM,), ((0, 2),), -0.2, 0.2)), 1.0, 2.0)
    video_key_gain = jnp.clip(jnp.exp(math.log(2.0) - 0.6931472 * jax.random.uniform(seeds[7], (VIDEO_HEADS * HEAD_DIM,), jnp.float32) ** steps_of(seeds[7], (VIDEO_HEADS * HEAD_DIM,), ((0, 2),), -0.2, 0.2)), 1.0, 2.0)
    audio_query_gain = jnp.clip(jnp.exp(math.log(2.0) - 0.6931472 * jax.random.uniform(seeds[8], (AUDIO_HEADS * HEAD_DIM,), jnp.float32) ** steps_of(seeds[8], (AUDIO_HEADS * HEAD_DIM,), ((0, 2),), -0.2, 0.2)), 1.0, 2.0)
    audio_key_gain = jnp.clip(jnp.exp(math.log(2.0) - 0.6931472 * jax.random.uniform(seeds[9], (AUDIO_HEADS * HEAD_DIM,), jnp.float32) ** steps_of(seeds[9], (AUDIO_HEADS * HEAD_DIM,), ((0, 2),), -0.2, 0.2)), 1.0, 2.0)
    return dict(video_q=video_q, video_k=video_k, video_v=video_v, audio_q=audio_q, audio_k=audio_k, audio_v=audio_v, video_query_gain=video_query_gain, video_key_gain=video_key_gain, audio_query_gain=audio_query_gain, audio_key_gain=audio_key_gain)


def softmax_attend(queries, key_rows, values, head_count):
    query_count = queries.shape[0]

    def per_head(index):
        offset = (index * HEAD_DIM).astype(jnp.int32)
        left = lax.dynamic_slice_in_dim(queries, offset, HEAD_DIM, 1)
        right = lax.dynamic_slice_in_dim(key_rows, offset, HEAD_DIM, 1)
        value_cols = lax.dynamic_slice_in_dim(values, offset, HEAD_DIM, 1)
        scores = jnp.dot(left, right.T, preferred_element_type=jnp.float32) * HEAD_DIM ** (-0.5)
        weights = jnp.exp(scores - lax.optimization_barrier(jnp.max(scores, axis=1, keepdims=True)))
        row_total = lax.optimization_barrier(jnp.sum(weights, axis=1))
        output = jnp.dot(weights.astype(jnp.bfloat16), value_cols, preferred_element_type=jnp.float32)
        return output / row_total[:, None]
    stacked = lax.map(per_head, jnp.arange(head_count, dtype=jnp.int32))
    return jnp.transpose(stacked, (1, 0, 2)).reshape(query_count, head_count * HEAD_DIM)

def normed(tokens, gain_row):
    count = tokens.shape[0]
    head_count = tokens.shape[1] // HEAD_DIM
    entries = tokens.astype(jnp.float32).reshape(count, head_count, HEAD_DIM)
    scaled = entries * lax.rsqrt(lax.optimization_barrier(jnp.mean(entries * entries, axis=2, keepdims=True)) + 1e-06)
    return (scaled.reshape(count, head_count * HEAD_DIM) * gain_row).astype(jnp.bfloat16)

def reference(video_q, video_k, video_v, audio_q, audio_k, audio_v, video_query_gain, video_key_gain, audio_query_gain, audio_key_gain):
    video_self = softmax_attend(video_q, video_k, video_v, VIDEO_HEADS).astype(jnp.bfloat16)
    audio_self = softmax_attend(audio_q, audio_k, audio_v, AUDIO_HEADS).astype(jnp.bfloat16)
    video_cross = softmax_attend(normed(video_self, video_query_gain), normed(audio_self, audio_key_gain), audio_self, VIDEO_HEADS)
    audio_cross = softmax_attend(normed(audio_self, audio_query_gain), normed(video_self, video_key_gain), video_self, AUDIO_HEADS)
    video_mixed = (video_self.astype(jnp.float32) + video_cross).astype(jnp.bfloat16)
    audio_mixed = (audio_self.astype(jnp.float32) + audio_cross).astype(jnp.bfloat16)
    return (video_mixed, audio_mixed)
```

```python
import functools
import math

import jax
import jax.numpy as jnp
from jax import lax
from jax.experimental import pallas as pl
from jax.experimental.pallas import tpu as pltpu
from jax.sharding import PartitionSpec as P

HEAD_DIM = 128
EXP2_SCALE = HEAD_DIM ** (-0.5) * math.log2(math.e)


def normed(tokens, gain_row):
    count = tokens.shape[0]
    head_count = tokens.shape[1] // HEAD_DIM
    entries = tokens.astype(jnp.float32).reshape(count, head_count, HEAD_DIM)
    scaled = entries * lax.rsqrt(jnp.mean(entries * entries, axis=2, keepdims=True) + 1e-06)
    return (scaled.reshape(count, head_count * HEAD_DIM) * gain_row).astype(jnp.bfloat16)


def start_state(row_count, head_count):
    return (
        jnp.full((head_count, row_count), -1e30, jnp.float32),
        jnp.zeros((head_count, row_count), jnp.float32),
        jnp.zeros((row_count, head_count, HEAD_DIM), jnp.float32),
    )


def folding(queries, prepare):
    head_count = queries.shape[1]

    def fold_step(state_now, pieces, offset):
        key_rows, values = prepare(pieces)
        key_rows = key_rows.reshape(key_rows.shape[0], head_count, HEAD_DIM)
        values = values.reshape(values.shape[0], head_count, HEAD_DIM)
        scores = jnp.einsum(
            "qhd,khd->hqk", queries, key_rows, preferred_element_type=jnp.float32
        ) * HEAD_DIM ** (-0.5)
        running_max, row_total, accumulated = state_now
        new_max = jnp.maximum(running_max, jnp.max(scores, axis=2))
        rescale = jnp.exp(running_max - new_max)
        weights = jnp.exp(scores - new_max[:, :, None])
        row_total = jnp.sum(weights, axis=2)
        update = jnp.einsum(
            "hqk,khd->qhd", weights.astype(jnp.bfloat16), values, preferred_element_type=jnp.float32
        )
        accumulated = accumulated * rescale.T[:, :, None] + update
        return (new_max, row_total, accumulated)

    return fold_step


def finish(state_now):
    running_max, row_total, accumulated = state_now
    result = accumulated / row_total.T[:, :, None]
    return result.reshape(result.shape[0], result.shape[1] * HEAD_DIM)


def as_heads(tokens):
    return tokens.reshape(tokens.shape[0], tokens.shape[1] // HEAD_DIM, HEAD_DIM)


def keep_pair(pieces):
    return pieces


def per_device(
    video_q,
    video_k,
    video_v,
    audio_q,
    audio_k,
    audio_v,
    video_query_gain,
    video_key_gain,
    audio_query_gain,
    audio_key_gain,
):
    head_count = video_q.shape[1] // HEAD_DIM
    video_rows = video_q.shape[0]
    audio_rows = audio_q.shape[0]
    video_state = folding(as_heads(video_q), keep_pair)(
        start_state(video_rows, head_count),
        (
            lax.all_gather(video_k, "seq", axis=0, tiled=True),
            lax.all_gather(video_v, "seq", axis=0, tiled=True),
        ),
        jnp.int32(0),
    )
    video_self = finish(video_state).astype(jnp.bfloat16)
    audio_state = folding(as_heads(audio_q), keep_pair)(
        start_state(audio_rows, head_count),
        (
            lax.all_gather(audio_k, "seq", axis=0, tiled=True),
            lax.all_gather(audio_v, "seq", axis=0, tiled=True),
        ),
        jnp.int32(0),
    )
    audio_self = finish(audio_state).astype(jnp.bfloat16)
    audio_whole = lax.all_gather(audio_self, "seq", axis=0, tiled=True)
    video_queries = as_heads(normed(video_self, video_query_gain))
    cross_step = folding(video_queries, keep_pair)
    video_cross = finish(
        cross_step(
            start_state(video_rows, head_count),
            (normed(audio_whole, audio_key_gain), audio_whole),
            0,
        )
    )
    audio_queries = normed(audio_self, audio_query_gain)

    def prepare_video(shard_rows):
        return (normed(shard_rows, video_key_gain), shard_rows)

    audio_state_cross = folding(as_heads(audio_queries), prepare_video)(
        start_state(audio_rows, head_count),
        lax.all_gather(video_self, "seq", axis=0, tiled=True),
        jnp.int32(0),
    )
    audio_cross = finish(audio_state_cross)
    video_mixed = (video_self.astype(jnp.float32) + video_cross).astype(jnp.bfloat16)
    audio_mixed = (audio_self.astype(jnp.float32) + audio_cross).astype(jnp.bfloat16)
    return (video_mixed, audio_mixed)


def attend_kernel(
    n,
    video_q,
    video_k,
    video_v,
    audio_q,
    audio_k,
    audio_v,
    video_query_gain,
    video_key_gain,
    audio_query_gain,
    audio_key_gain,
    video_out,
    audio_out,
    vq,
    vk,
    vv,
    aq,
    ak,
    av,
    video_self,
    audio_self,
    audio_queries,
    audio_keys,
    audio_sum,
    video_mixed,
    audio_mixed,
    send_sem,
    recv_sem,
    own_sem,
    out_send_sem,
    out_recv_sem,
    out_own_sem,
):
    me = lax.axis_index("seq")
    rows = video_q.shape[0]
    arows = audio_q.shape[0]

    def peer_of(step, sign):
        distance = lax.select(step % 2 == 1, (step + 1) // 2, n - step // 2)
        return lax.rem(me + n + sign * distance, n)

    def head_columns(index):
        return pl.ds(pl.multiple_of(index * HEAD_DIM, HEAD_DIM), HEAD_DIM)

    def token_rows(index, count):
        return pl.ds(pl.multiple_of(index * count, count), count)

    ins = (
        (audio_k, ak, arows),
        (audio_v, av, arows),
        (audio_q, aq, arows),
        (video_k, vk, rows),
        (video_v, vv, rows),
        (video_q, vq, rows),
    )

    def own_in(kind):
        source, target, count = ins[kind]
        return pltpu.make_async_copy(
            source.at[:, head_columns(me)],
            target.at[token_rows(me, count), pl.ds(0, HEAD_DIM)],
            own_sem.at[kind],
        )

    def sent_in(kind, peer):
        source, target, count = ins[kind]
        return pltpu.make_async_remote_copy(
            src_ref=source.at[:, head_columns(peer)],
            dst_ref=target.at[token_rows(me, count), pl.ds(0, HEAD_DIM)],
            send_sem=send_sem.at[kind, peer],
            recv_sem=recv_sem.at[kind, me],
            device_id={"seq": peer},
            device_id_type=pl.DeviceIdType.MESH,
        )

    def received_in(kind, peer):
        source, target, count = ins[kind]
        return pltpu.make_async_remote_copy(
            src_ref=source.at[:, head_columns(peer)],
            dst_ref=target.at[token_rows(peer, count), pl.ds(0, HEAD_DIM)],
            send_sem=send_sem.at[kind, peer],
            recv_sem=recv_sem.at[kind, peer],
            device_id={"seq": peer},
            device_id_type=pl.DeviceIdType.MESH,
        )

    outs = ((audio_mixed, audio_out, arows), (video_mixed, video_out, rows))

    def own_out(kind):
        source, target, count = outs[kind]
        return pltpu.make_async_copy(
            source.at[token_rows(me, count), :],
            target.at[:, head_columns(me)],
            out_own_sem.at[kind],
        )

    def sent_out(kind, peer):
        source, target, count = outs[kind]
        return pltpu.make_async_remote_copy(
            src_ref=source.at[token_rows(peer, count), :],
            dst_ref=target.at[:, head_columns(me)],
            send_sem=out_send_sem.at[kind, peer],
            recv_sem=out_recv_sem.at[kind, me],
            device_id={"seq": peer},
            device_id_type=pl.DeviceIdType.MESH,
        )

    def received_out(kind, peer):
        source, target, count = outs[kind]
        return pltpu.make_async_remote_copy(
            src_ref=source.at[token_rows(peer, count), :],
            dst_ref=target.at[:, head_columns(peer)],
            send_sem=out_send_sem.at[kind, peer],
            recv_sem=out_recv_sem.at[kind, peer],
            device_id={"seq": peer},
            device_id_type=pl.DeviceIdType.MESH,
        )

    for kind in range(len(ins)):
        own_in(kind).start()

    barrier = pltpu.get_barrier_semaphore()
    for step in range(1, n):
        pl.semaphore_signal(
            barrier,
            inc=1,
            device_id={"seq": lax.rem(me + step, n)},
            device_id_type=pl.DeviceIdType.MESH,
        )
    pl.semaphore_wait(barrier, n - 1)

    for kinds in SEND_ORDER:

        def send_step(step, carry, kinds=kinds):
            for kind in kinds:
                sent_in(kind, peer_of(step, 1)).start()
            return carry

        lax.fori_loop(1, n, send_step, 0)

    ones = jnp.ones((arows * n, HEAD_DIM), jnp.bfloat16)
    av[:, HEAD_DIM:] = ones
    audio_self[:, HEAD_DIM:] = ones
    ones = jnp.ones((rows * n, HEAD_DIM), jnp.bfloat16)
    vv[:, HEAD_DIM:] = ones
    video_self[:, HEAD_DIM:] = ones
    audio_sum[...] = jnp.zeros_like(audio_sum)

    def wait_kinds(kinds):
        for kind in kinds:
            own_in(kind).wait()

        def wait_step(step, carry):
            for kind in kinds:
                received_in(kind, peer_of(step, -1)).wait_recv()
            return carry

        lax.fori_loop(1, n, wait_step, 0)

    def dot_t(left, right):
        return lax.dot_general(
            left, right, (((1,), (1,)), ((), ())), preferred_element_type=jnp.float32
        )

    def dot(left, right):
        return jnp.dot(left, right, preferred_element_type=jnp.float32)

    def self_attend(queries, key_rows, values):
        scores = dot_t(queries, key_rows)
        largest = jnp.max(scores, axis=1, keepdims=True)
        weights = jnp.exp2((scores - largest) * EXP2_SCALE).astype(jnp.bfloat16)
        both = dot(weights, values)
        return (both[:, :HEAD_DIM] / both[:, HEAD_DIM:]).astype(jnp.bfloat16)

    def unit(tokens):
        entries = tokens.astype(jnp.float32)
        mean = jnp.mean(entries * entries, axis=1, keepdims=True)
        return entries * lax.rsqrt(mean + 1e-06)

    own_head = pl.ds(me, 1)
    wait_kinds((0, 1, 2))
    tokens = self_attend(aq[...], ak[...], av[...])
    audio_self[:, :HEAD_DIM] = tokens
    scaled = unit(tokens)
    audio_queries[...] = (scaled * audio_query_gain[own_head, :]).astype(jnp.bfloat16)
    audio_keys[...] = (scaled * audio_key_gain[own_head, :]).astype(jnp.bfloat16)

    wait_kinds((3, 4))

    def video_block(peer):
        here = token_rows(peer, rows)
        tokens = self_attend(vq[here, :], vk[...], vv[...])
        video_self[here, :HEAD_DIM] = tokens
        scaled = unit(tokens)
        queries = (scaled * video_query_gain[own_head, :]).astype(jnp.bfloat16)
        key_rows = (scaled * video_key_gain[own_head, :]).astype(jnp.bfloat16)
        weights = jnp.exp2(dot_t(queries, audio_keys[...]) * EXP2_SCALE)
        both = dot(weights.astype(jnp.bfloat16), audio_self[...])
        cross = both[:, :HEAD_DIM] / both[:, HEAD_DIM:]
        video_mixed[here, :] = (tokens.astype(jnp.float32) + cross).astype(jnp.bfloat16)
        weights = jnp.exp2(dot_t(audio_queries[...], key_rows) * EXP2_SCALE)
        audio_sum[...] += dot(weights.astype(jnp.bfloat16), video_self[here, :])

    own_in(5).wait()
    video_block(me)
    own_out(1).start()

    def block_step(step, carry):
        peer = peer_of(step, -1)
        received_in(5, peer).wait_recv()
        video_block(peer)
        sent_out(1, peer).start()
        return carry

    lax.fori_loop(1, n, block_step, 0)

    both = audio_sum[...]
    cross = both[:, :HEAD_DIM] / both[:, HEAD_DIM:]
    audio_mixed[...] = (audio_self[:, :HEAD_DIM].astype(jnp.float32) + cross).astype(jnp.bfloat16)
    own_out(0).start()

    def send_audio(step, carry):
        sent_out(0, peer_of(step, 1)).start()
        return carry

    lax.fori_loop(1, n, send_audio, 0)

    def finish_step(step, carry):
        peer = peer_of(step, 1)
        for kind in range(len(ins)):
            sent_in(kind, peer).wait_send()
        for kind in range(len(outs)):
            sent_out(kind, peer).wait_send()
            received_out(kind, peer).wait_recv()
        return carry

    lax.fori_loop(1, n, finish_step, 0)
    own_out(0).wait()
    own_out(1).wait()


SEND_ORDER = ((0, 1, 2), (3, 4), (5,))


def head_per_device(n, *arrays):
    video_q, audio_q = arrays[0], arrays[3]
    tokens, atokens = video_q.shape[0] * n, audio_q.shape[0] * n
    bf16, f32 = jnp.bfloat16, jnp.float32
    gains = [gain.reshape(n, HEAD_DIM) for gain in arrays[6:]]
    anywhere = pl.BlockSpec(memory_space=pl.ANY)
    vmem = pl.BlockSpec(memory_space=pltpu.VMEM)
    return pl.pallas_call(
        functools.partial(attend_kernel, n),
        out_shape=(
            jax.ShapeDtypeStruct(video_q.shape, bf16),
            jax.ShapeDtypeStruct(audio_q.shape, bf16),
        ),
        in_specs=[anywhere] * 6 + [vmem] * 4,
        out_specs=(anywhere, anywhere),
        scratch_shapes=[
            pltpu.VMEM((tokens, HEAD_DIM), bf16),
            pltpu.VMEM((tokens, HEAD_DIM), bf16),
            pltpu.VMEM((tokens, 2 * HEAD_DIM), bf16),
            pltpu.VMEM((atokens, HEAD_DIM), bf16),
            pltpu.VMEM((atokens, HEAD_DIM), bf16),
            pltpu.VMEM((atokens, 2 * HEAD_DIM), bf16),
            pltpu.VMEM((tokens, 2 * HEAD_DIM), bf16),
            pltpu.VMEM((atokens, 2 * HEAD_DIM), bf16),
            pltpu.VMEM((atokens, HEAD_DIM), bf16),
            pltpu.VMEM((atokens, HEAD_DIM), bf16),
            pltpu.VMEM((atokens, 2 * HEAD_DIM), f32),
            pltpu.VMEM((tokens, HEAD_DIM), bf16),
            pltpu.VMEM((atokens, HEAD_DIM), bf16),
            pltpu.SemaphoreType.DMA((6, n)),
            pltpu.SemaphoreType.DMA((6, n)),
            pltpu.SemaphoreType.DMA((6,)),
            pltpu.SemaphoreType.DMA((2, n)),
            pltpu.SemaphoreType.DMA((2, n)),
            pltpu.SemaphoreType.DMA((2,)),
        ],
        compiler_params=pltpu.CompilerParams(collective_id=0, has_side_effects=True),
    )(*arrays[:6], *gains)


def solution(mesh):
    in_specs = (
        P(("clips", "seq"), "head"),
        P(("clips", "seq"), "head"),
        P(("clips", "seq"), "head"),
        P(("clips", "seq"), "head"),
        P(("clips", "seq"), "head"),
        P(("clips", "seq"), "head"),
        P("head"),
        P("head"),
        P("head"),
        P("head"),
    )
    out_specs = (P(("clips", "seq"), "head"), P(("clips", "seq"), "head"))
    sizes = dict(mesh.shape)

    def body(*arrays):
        video_q, audio_q = arrays[0], arrays[3]
        if (
            video_q.shape[1] == sizes["seq"] * HEAD_DIM
            and video_q.shape[0] % 16 == 0
            and audio_q.shape[0] % 16 == 0
        ):
            return head_per_device(sizes["seq"], *arrays)
        return per_device(*arrays)

    return jax.shard_map(
        body, mesh=mesh, in_specs=in_specs, out_specs=out_specs, check_vma=False
    )
```

```python
import functools
import math

import jax
import jax.numpy as jnp
from jax import lax
from jax.experimental import pallas as pl
from jax.experimental.pallas import tpu as pltpu
from jax.sharding import PartitionSpec as P

HEAD_DIM = 128
EXP2_SCALE = HEAD_DIM ** (-0.5) * math.log2(math.e)


def normed(tokens, gain_row):
    count = tokens.shape[0]
    head_count = tokens.shape[1] // HEAD_DIM
    entries = tokens.astype(jnp.float32).reshape(count, head_count, HEAD_DIM)
    scaled = entries * lax.rsqrt(jnp.mean(entries * entries, axis=2, keepdims=True) + 1e-06)
    return (scaled.reshape(count, head_count * HEAD_DIM) * gain_row).astype(jnp.bfloat16)


def start_state(row_count, head_count):
    return (
        jnp.full((head_count, row_count), -1e30, jnp.float32),
        jnp.zeros((head_count, row_count), jnp.float32),
        jnp.zeros((row_count, head_count, HEAD_DIM), jnp.float32),
    )


def folding(queries, prepare):
    head_count = queries.shape[1]

    def fold_step(state_now, pieces, offset):
        key_rows, values = prepare(pieces)
        key_rows = key_rows.reshape(key_rows.shape[0], head_count, HEAD_DIM)
        values = values.reshape(values.shape[0], head_count, HEAD_DIM)
        scores = jnp.einsum(
            "qhd,khd->hqk", queries, key_rows, preferred_element_type=jnp.float32
        ) * HEAD_DIM ** (-0.5)
        running_max, row_total, accumulated = state_now
        new_max = jnp.maximum(running_max, jnp.max(scores, axis=2))
        rescale = jnp.exp(running_max - new_max)
        weights = jnp.exp(scores - new_max[:, :, None])
        row_total = jnp.sum(weights, axis=2)
        update = jnp.einsum(
            "hqk,khd->qhd", weights.astype(jnp.bfloat16), values, preferred_element_type=jnp.float32
        )
        accumulated = accumulated * rescale.T[:, :, None] + update
        return (new_max, row_total, accumulated)

    return fold_step


def finish(state_now):
    running_max, row_total, accumulated = state_now
    result = accumulated / row_total.T[:, :, None]
    return result.reshape(result.shape[0], result.shape[1] * HEAD_DIM)


def as_heads(tokens):
    return tokens.reshape(tokens.shape[0], tokens.shape[1] // HEAD_DIM, HEAD_DIM)


def keep_pair(pieces):
    return pieces


def per_device(
    video_q,
    video_k,
    video_v,
    audio_q,
    audio_k,
    audio_v,
    video_query_gain,
    video_key_gain,
    audio_query_gain,
    audio_key_gain,
):
    head_count = video_q.shape[1] // HEAD_DIM
    video_rows = video_q.shape[0]
    audio_rows = audio_q.shape[0]
    video_state = folding(as_heads(video_q), keep_pair)(
        start_state(video_rows, head_count),
        (
            lax.all_gather(video_k, "seq", axis=0, tiled=True),
            lax.all_gather(video_v, "seq", axis=0, tiled=True),
        ),
        jnp.int32(0),
    )
    video_self = finish(video_state).astype(jnp.bfloat16)
    audio_state = folding(as_heads(audio_q), keep_pair)(
        start_state(audio_rows, head_count),
        (
            lax.all_gather(audio_k, "seq", axis=0, tiled=True),
            lax.all_gather(audio_v, "seq", axis=0, tiled=True),
        ),
        jnp.int32(0),
    )
    audio_self = finish(audio_state).astype(jnp.bfloat16)
    audio_whole = lax.all_gather(audio_self, "seq", axis=0, tiled=True)
    video_queries = as_heads(normed(video_self, video_query_gain))
    cross_step = folding(video_queries, keep_pair)
    video_cross = finish(
        cross_step(
            start_state(video_rows, head_count),
            (normed(audio_whole, audio_key_gain), audio_whole),
            0,
        )
    )
    audio_queries = normed(audio_self, audio_query_gain)

    def prepare_video(shard_rows):
        return (normed(shard_rows, video_key_gain), shard_rows)

    audio_state_cross = folding(as_heads(audio_queries), prepare_video)(
        start_state(audio_rows, head_count),
        lax.all_gather(video_self, "seq", axis=0, tiled=True),
        jnp.int32(0),
    )
    audio_cross = finish(audio_state_cross)
    video_mixed = (video_self.astype(jnp.float32) + video_cross).astype(jnp.bfloat16)
    audio_mixed = (audio_self.astype(jnp.float32) + audio_cross).astype(jnp.bfloat16)
    return (video_mixed, audio_mixed)


def attend_kernel(
    n,
    video_q,
    video_k,
    video_v,
    audio_q,
    audio_k,
    audio_v,
    video_query_gain,
    video_key_gain,
    audio_query_gain,
    audio_key_gain,
    video_out,
    audio_out,
    vq,
    vk,
    vv,
    aq,
    ak,
    av,
    audio_self,
    audio_queries,
    audio_keys,
    audio_sum,
    video_mixed,
    audio_mixed,
    send_sem,
    recv_sem,
    own_sem,
    out_send_sem,
    out_recv_sem,
    out_own_sem,
):
    me = lax.axis_index("seq")
    rows = video_q.shape[0]
    arows = audio_q.shape[0]

    half = n // 2 if n % 2 == 0 else n
    far_count = n - half

    def near_peer(step, sign):
        return me // half * half + lax.rem(lax.rem(me, half) + half + sign * step, half)

    def far_peer(step, sign):
        return lax.rem(near_peer(step, sign) + half, n)

    def over_peers(visit, sign, far_first):
        def far(step, carry):
            visit(far_peer(step, sign))
            return carry

        def near(step, carry):
            visit(near_peer(step, sign))
            return carry

        if far_first:
            lax.fori_loop(0, far_count, far, 0)
        lax.fori_loop(1, half, near, 0)
        if not far_first:
            lax.fori_loop(0, far_count, far, 0)

    def head_columns(index):
        return pl.ds(pl.multiple_of(index * HEAD_DIM, HEAD_DIM), HEAD_DIM)

    def token_rows(index, count):
        return pl.ds(pl.multiple_of(index * count, count), count)

    ins = (
        (audio_k, ak, arows),
        (audio_v, av, arows),
        (audio_q, aq, arows),
        (video_k, vk, rows),
        (video_v, vv, rows),
        (video_q, vq, rows),
    )

    def own_in(kind):
        source, target, count = ins[kind]
        return pltpu.make_async_copy(
            source.at[:, head_columns(me)],
            target.at[token_rows(me, count), pl.ds(0, HEAD_DIM)],
            own_sem.at[kind],
        )

    def sent_in(kind, peer):
        source, target, count = ins[kind]
        return pltpu.make_async_remote_copy(
            src_ref=source.at[:, head_columns(peer)],
            dst_ref=target.at[token_rows(me, count), pl.ds(0, HEAD_DIM)],
            send_sem=send_sem.at[kind, peer],
            recv_sem=recv_sem.at[kind, me],
            device_id={"seq": peer},
            device_id_type=pl.DeviceIdType.MESH,
        )

    def received_in(kind, peer):
        source, target, count = ins[kind]
        return pltpu.make_async_remote_copy(
            src_ref=source.at[:, head_columns(peer)],
            dst_ref=target.at[token_rows(peer, count), pl.ds(0, HEAD_DIM)],
            send_sem=send_sem.at[kind, peer],
            recv_sem=recv_sem.at[kind, peer],
            device_id={"seq": peer},
            device_id_type=pl.DeviceIdType.MESH,
        )

    outs = ((audio_mixed, audio_out, arows), (video_mixed, video_out, rows))

    def own_out(kind):
        source, target, count = outs[kind]
        return pltpu.make_async_copy(
            source.at[token_rows(me, count), :],
            target.at[:, head_columns(me)],
            out_own_sem.at[kind],
        )

    def sent_out(kind, peer):
        source, target, count = outs[kind]
        return pltpu.make_async_remote_copy(
            src_ref=source.at[token_rows(peer, count), :],
            dst_ref=target.at[:, head_columns(me)],
            send_sem=out_send_sem.at[kind, peer],
            recv_sem=out_recv_sem.at[kind, me],
            device_id={"seq": peer},
            device_id_type=pl.DeviceIdType.MESH,
        )

    def received_out(kind, peer):
        source, target, count = outs[kind]
        return pltpu.make_async_remote_copy(
            src_ref=source.at[token_rows(peer, count), :],
            dst_ref=target.at[:, head_columns(peer)],
            send_sem=out_send_sem.at[kind, peer],
            recv_sem=out_recv_sem.at[kind, peer],
            device_id={"seq": peer},
            device_id_type=pl.DeviceIdType.MESH,
        )

    for kind in range(len(ins)):
        own_in(kind).start()

    barrier = pltpu.get_barrier_semaphore()
    for step in range(1, n):
        pl.semaphore_signal(
            barrier,
            inc=1,
            device_id={"seq": lax.rem(me + step, n)},
            device_id_type=pl.DeviceIdType.MESH,
        )
    pl.semaphore_wait(barrier, n - 1)

    for kinds, far_first in SEND_ORDER:

        def send_kinds(peer, kinds=kinds):
            for kind in kinds:
                sent_in(kind, peer).start()

        over_peers(send_kinds, 1, far_first)

    ones = jnp.ones((arows * n, HEAD_DIM), jnp.bfloat16)
    av[:, HEAD_DIM:] = ones
    audio_self[:, HEAD_DIM:] = ones
    ones = jnp.ones((rows * n, HEAD_DIM), jnp.bfloat16)
    vv[:, HEAD_DIM:] = ones
    audio_sum[...] = jnp.zeros_like(audio_sum)

    def wait_kinds(kinds):
        for kind in kinds:
            own_in(kind).wait()

        def wait_peer(peer):
            for kind in kinds:
                received_in(kind, peer).wait_recv()

        over_peers(wait_peer, -1, False)

    def dot_t(left, right):
        return lax.dot_general(
            left, right, (((1,), (1,)), ((), ())), preferred_element_type=jnp.float32
        )

    def dot(left, right):
        return jnp.dot(left, right, preferred_element_type=jnp.float32)

    def self_attend(queries, key_rows, values):
        scores = dot_t(queries, key_rows)
        largest = jnp.max(scores, axis=1, keepdims=True)
        weights = jnp.exp2((scores - largest) * EXP2_SCALE).astype(jnp.bfloat16)
        both = dot(weights, values)
        return (both[:, :HEAD_DIM] / both[:, HEAD_DIM:]).astype(jnp.bfloat16)

    def unit(tokens):
        entries = tokens.astype(jnp.float32)
        mean = jnp.mean(entries * entries, axis=1, keepdims=True)
        return entries * lax.rsqrt(mean + 1e-06)

    own_head = pl.ds(me, 1)
    wait_kinds((0, 1, 2))
    tokens = self_attend(aq[...], ak[...], av[...])
    audio_self[:, :HEAD_DIM] = tokens
    scaled = unit(tokens)
    audio_queries[...] = (scaled * audio_query_gain[own_head, :]).astype(jnp.bfloat16)
    audio_keys[...] = (scaled * audio_key_gain[own_head, :]).astype(jnp.bfloat16)

    wait_kinds((3, 4))

    def self_part(peers):
        here = [token_rows(peer, rows) for peer in peers]
        tokens = self_attend(jnp.concatenate([vq[one, :] for one in here], 0), vk[...], vv[...])
        scaled = unit(tokens)
        queries = (scaled * video_query_gain[own_head, :]).astype(jnp.bfloat16)
        key_rows = (scaled * video_key_gain[own_head, :]).astype(jnp.bfloat16)
        return tokens, queries, key_rows

    def audio_part(tokens, key_rows):
        weights = jnp.exp2(dot_t(audio_queries[...], key_rows) * EXP2_SCALE)
        values = jnp.concatenate([tokens, jnp.ones_like(tokens)], 1)
        audio_sum[...] += dot(weights.astype(jnp.bfloat16), values)

    def video_part(peers, tokens, queries):
        weights = jnp.exp2(dot_t(queries, audio_keys[...]) * EXP2_SCALE)
        both = dot(weights.astype(jnp.bfloat16), audio_self[...])
        cross = both[:, :HEAD_DIM] / both[:, HEAD_DIM:]
        mixed = (tokens.astype(jnp.float32) + cross).astype(jnp.bfloat16)
        for index, peer in enumerate(peers):
            video_mixed[token_rows(peer, rows), :] = mixed[index * rows : (index + 1) * rows]

    def send_audio(peer):
        sent_out(0, peer).start()

    others = [far_peer(step, -1) for step in range(far_count)]
    others += [near_peer(step, -1) for step in range(1, half)]
    group = GROUP if n % GROUP == 0 else 1
    for first in range(0, n, group):
        last = first + group == n
        here = others[first : first + group]
        for peer in here:
            received_in(5, peer).wait_recv()
        if last:
            own_in(5).wait()
        peers = here + [me] if last else here
        tokens, queries, key_rows = self_part(peers)
        if not last:
            video_part(peers, tokens, queries)
            for peer in here:
                sent_out(1, peer).start()
            audio_part(tokens, key_rows)
        else:
            audio_part(tokens, key_rows)
            both = audio_sum[...]
            cross = both[:, :HEAD_DIM] / both[:, HEAD_DIM:]
            audio_mixed[...] = (
                audio_self[:, :HEAD_DIM].astype(jnp.float32) + cross
            ).astype(jnp.bfloat16)
            own_out(0).start()
            over_peers(send_audio, 1, True)
            video_part(peers, tokens, queries)
            for peer in here:
                sent_out(1, peer).start()
            own_out(1).start()

    def finish_peer(peer):
        for kind in range(len(ins)):
            sent_in(kind, peer).wait_send()
        for kind in range(len(outs)):
            sent_out(kind, peer).wait_send()
            received_out(kind, peer).wait_recv()

    over_peers(finish_peer, 1, True)
    own_out(0).wait()
    own_out(1).wait()


def pass_on_kernel(
    video_in, audio_in, video_out, audio_out, video_held, audio_held, in_sem, out_sem
):
    loads, stores = [], []
    for kind, (source, held, target) in enumerate(
        ((video_in, video_held, video_out), (audio_in, audio_held, audio_out))
    ):
        piece = source.shape[1] // PIECES
        for index in range(PIECES):
            here = (slice(None), pl.ds(index * piece, piece))
            loads.append(
                pltpu.make_async_copy(source.at[here], held.at[here], in_sem.at[kind, index])
            )
            stores.append(
                pltpu.make_async_copy(held.at[here], target.at[here], out_sem.at[kind, index])
            )
    for load in loads:
        load.start()
    for load, store in zip(loads, stores):
        load.wait()
        store.start()
    for store in stores:
        store.wait()


PIECES = 2
GROUP = 2
SEND_ORDER = (((0, 1, 2), False), ((3, 4), False), ((5,), True))


def head_per_device(n, *arrays):
    video_q, audio_q = arrays[0], arrays[3]
    tokens, atokens = video_q.shape[0] * n, audio_q.shape[0] * n
    bf16, f32 = jnp.bfloat16, jnp.float32
    gains = [gain.reshape(n, HEAD_DIM) for gain in arrays[6:]]
    anywhere = pl.BlockSpec(memory_space=pl.ANY)
    vmem = pl.BlockSpec(memory_space=pltpu.VMEM)
    results = pl.pallas_call(
        functools.partial(attend_kernel, n),
        out_shape=(
            jax.ShapeDtypeStruct(video_q.shape, bf16),
            jax.ShapeDtypeStruct(audio_q.shape, bf16),
        ),
        in_specs=[anywhere] * 6 + [vmem] * 4,
        out_specs=(anywhere, anywhere),
        scratch_shapes=[
            pltpu.VMEM((tokens, HEAD_DIM), bf16),
            pltpu.VMEM((tokens, HEAD_DIM), bf16),
            pltpu.VMEM((tokens, 2 * HEAD_DIM), bf16),
            pltpu.VMEM((atokens, HEAD_DIM), bf16),
            pltpu.VMEM((atokens, HEAD_DIM), bf16),
            pltpu.VMEM((atokens, 2 * HEAD_DIM), bf16),
            pltpu.VMEM((atokens, 2 * HEAD_DIM), bf16),
            pltpu.VMEM((atokens, HEAD_DIM), bf16),
            pltpu.VMEM((atokens, HEAD_DIM), bf16),
            pltpu.VMEM((atokens, 2 * HEAD_DIM), f32),
            pltpu.VMEM((tokens, HEAD_DIM), bf16),
            pltpu.VMEM((atokens, HEAD_DIM), bf16),
            pltpu.SemaphoreType.DMA((6, n)),
            pltpu.SemaphoreType.DMA((6, n)),
            pltpu.SemaphoreType.DMA((6,)),
            pltpu.SemaphoreType.DMA((2, n)),
            pltpu.SemaphoreType.DMA((2, n)),
            pltpu.SemaphoreType.DMA((2,)),
        ],
        compiler_params=pltpu.CompilerParams(collective_id=0, has_side_effects=True),
    )(*arrays[:6], *gains)
    return pl.pallas_call(
        pass_on_kernel,
        out_shape=(
            jax.ShapeDtypeStruct(video_q.shape, bf16),
            jax.ShapeDtypeStruct(audio_q.shape, bf16),
        ),
        in_specs=[anywhere] * 2,
        out_specs=(anywhere, anywhere),
        scratch_shapes=[
            pltpu.VMEM(video_q.shape, bf16),
            pltpu.VMEM(audio_q.shape, bf16),
            pltpu.SemaphoreType.DMA((2, PIECES)),
            pltpu.SemaphoreType.DMA((2, PIECES)),
        ],
    )(*results)


def solution(mesh):
    in_specs = (
        P(("clips", "seq"), "head"),
        P(("clips", "seq"), "head"),
        P(("clips", "seq"), "head"),
        P(("clips", "seq"), "head"),
        P(("clips", "seq"), "head"),
        P(("clips", "seq"), "head"),
        P("head"),
        P("head"),
        P("head"),
        P("head"),
    )
    out_specs = (P(("clips", "seq"), "head"), P(("clips", "seq"), "head"))
    sizes = dict(mesh.shape)

    def body(*arrays):
        video_q, audio_q = arrays[0], arrays[3]
        if (
            video_q.shape[1] == sizes["seq"] * HEAD_DIM
            and video_q.shape[0] % 16 == 0
            and audio_q.shape[0] % 16 == 0
        ):
            return head_per_device(sizes["seq"], *arrays)
        return per_device(*arrays)

    return jax.shard_map(
        body, mesh=mesh, in_specs=in_specs, out_specs=out_specs, check_vma=False
    )
```

```python
import functools
import math

import jax
import jax.numpy as jnp
from jax import lax
from jax.experimental import pallas as pl
from jax.experimental.pallas import tpu as pltpu
from jax.sharding import PartitionSpec as P

HEAD_DIM = 128
EXP2_SCALE = HEAD_DIM ** (-0.5) * math.log2(math.e)


def normed(tokens, gain_row):
    count = tokens.shape[0]
    head_count = tokens.shape[1] // HEAD_DIM
    entries = tokens.astype(jnp.float32).reshape(count, head_count, HEAD_DIM)
    scaled = entries * lax.rsqrt(jnp.mean(entries * entries, axis=2, keepdims=True) + 1e-06)
    return (scaled.reshape(count, head_count * HEAD_DIM) * gain_row).astype(jnp.bfloat16)


def start_state(row_count, head_count):
    return (
        jnp.full((head_count, row_count), -1e30, jnp.float32),
        jnp.zeros((head_count, row_count), jnp.float32),
        jnp.zeros((row_count, head_count, HEAD_DIM), jnp.float32),
    )


def folding(queries, prepare):
    head_count = queries.shape[1]

    def fold_step(state_now, pieces, offset):
        key_rows, values = prepare(pieces)
        key_rows = key_rows.reshape(key_rows.shape[0], head_count, HEAD_DIM)
        values = values.reshape(values.shape[0], head_count, HEAD_DIM)
        scores = jnp.einsum(
            "qhd,khd->hqk", queries, key_rows, preferred_element_type=jnp.float32
        ) * HEAD_DIM ** (-0.5)
        running_max, row_total, accumulated = state_now
        new_max = jnp.maximum(running_max, jnp.max(scores, axis=2))
        rescale = jnp.exp(running_max - new_max)
        weights = jnp.exp(scores - new_max[:, :, None])
        row_total = jnp.sum(weights, axis=2)
        update = jnp.einsum(
            "hqk,khd->qhd", weights.astype(jnp.bfloat16), values, preferred_element_type=jnp.float32
        )
        accumulated = accumulated * rescale.T[:, :, None] + update
        return (new_max, row_total, accumulated)

    return fold_step


def finish(state_now):
    running_max, row_total, accumulated = state_now
    result = accumulated / row_total.T[:, :, None]
    return result.reshape(result.shape[0], result.shape[1] * HEAD_DIM)


def as_heads(tokens):
    return tokens.reshape(tokens.shape[0], tokens.shape[1] // HEAD_DIM, HEAD_DIM)


def keep_pair(pieces):
    return pieces


def per_device(
    video_q,
    video_k,
    video_v,
    audio_q,
    audio_k,
    audio_v,
    video_query_gain,
    video_key_gain,
    audio_query_gain,
    audio_key_gain,
):
    head_count = video_q.shape[1] // HEAD_DIM
    video_rows = video_q.shape[0]
    audio_rows = audio_q.shape[0]
    video_state = folding(as_heads(video_q), keep_pair)(
        start_state(video_rows, head_count),
        (
            lax.all_gather(video_k, "seq", axis=0, tiled=True),
            lax.all_gather(video_v, "seq", axis=0, tiled=True),
        ),
        jnp.int32(0),
    )
    video_self = finish(video_state).astype(jnp.bfloat16)
    audio_state = folding(as_heads(audio_q), keep_pair)(
        start_state(audio_rows, head_count),
        (
            lax.all_gather(audio_k, "seq", axis=0, tiled=True),
            lax.all_gather(audio_v, "seq", axis=0, tiled=True),
        ),
        jnp.int32(0),
    )
    audio_self = finish(audio_state).astype(jnp.bfloat16)
    audio_whole = lax.all_gather(audio_self, "seq", axis=0, tiled=True)
    video_queries = as_heads(normed(video_self, video_query_gain))
    cross_step = folding(video_queries, keep_pair)
    video_cross = finish(
        cross_step(
            start_state(video_rows, head_count),
            (normed(audio_whole, audio_key_gain), audio_whole),
            0,
        )
    )
    audio_queries = normed(audio_self, audio_query_gain)

    def prepare_video(shard_rows):
        return (normed(shard_rows, video_key_gain), shard_rows)

    audio_state_cross = folding(as_heads(audio_queries), prepare_video)(
        start_state(audio_rows, head_count),
        lax.all_gather(video_self, "seq", axis=0, tiled=True),
        jnp.int32(0),
    )
    audio_cross = finish(audio_state_cross)
    video_mixed = (video_self.astype(jnp.float32) + video_cross).astype(jnp.bfloat16)
    audio_mixed = (audio_self.astype(jnp.float32) + audio_cross).astype(jnp.bfloat16)
    return (video_mixed, audio_mixed)


def attend_kernel(
    n,
    video_q,
    video_k,
    video_v,
    audio_q,
    audio_k,
    audio_v,
    video_query_gain,
    video_key_gain,
    audio_query_gain,
    audio_key_gain,
    video_out,
    audio_out,
    vq,
    vk,
    vv,
    aq,
    ak,
    av,
    audio_self,
    audio_queries,
    audio_keys,
    audio_sum,
    video_mixed,
    audio_mixed,
    send_sem,
    recv_sem,
    own_sem,
    out_send_sem,
    out_recv_sem,
    out_own_sem,
    far_in_sem,
):
    me = lax.axis_index("seq")
    rows = video_q.shape[0]
    arows = audio_q.shape[0]

    half = n // 2 if n % 2 == 0 else n
    far_count = n - half

    def near_peer(step, sign):
        return me // half * half + lax.rem(lax.rem(me, half) + half + sign * step, half)

    def far_peer(step, sign):
        return lax.rem(near_peer(step, sign) + half, n)

    def over_peers(visit, sign, far_first):
        def far(step, carry):
            visit(far_peer(step, sign))
            return carry

        def near(step, carry):
            visit(near_peer(step, sign))
            return carry

        if far_first:
            lax.fori_loop(0, far_count, far, 0)
        lax.fori_loop(1, half, near, 0)
        if not far_first:
            lax.fori_loop(0, far_count, far, 0)

    def head_columns(index):
        return pl.ds(pl.multiple_of(index * HEAD_DIM, HEAD_DIM), HEAD_DIM)

    def token_rows(index, count):
        return pl.ds(pl.multiple_of(index * count, count), count)

    ins = (
        (audio_k, ak, arows),
        (audio_v, av, arows),
        (audio_q, aq, arows),
        (video_k, vk, rows),
        (video_v, vv, rows),
        (video_q, vq, rows),
    )

    def own_in(kind):
        source, target, count = ins[kind]
        return pltpu.make_async_copy(
            source.at[:, head_columns(me)],
            target.at[token_rows(me, count), pl.ds(0, HEAD_DIM)],
            own_sem.at[kind],
        )

    def sent_in(kind, peer):
        source, target, count = ins[kind]
        return pltpu.make_async_remote_copy(
            src_ref=source.at[:, head_columns(peer)],
            dst_ref=target.at[token_rows(me, count), pl.ds(0, HEAD_DIM)],
            send_sem=send_sem.at[kind, peer],
            recv_sem=recv_sem.at[kind, me],
            device_id={"seq": peer},
            device_id_type=pl.DeviceIdType.MESH,
        )

    def received_in(kind, peer):
        source, target, count = ins[kind]
        return pltpu.make_async_remote_copy(
            src_ref=source.at[:, head_columns(peer)],
            dst_ref=target.at[token_rows(peer, count), pl.ds(0, HEAD_DIM)],
            send_sem=send_sem.at[kind, peer],
            recv_sem=recv_sem.at[kind, peer],
            device_id={"seq": peer},
            device_id_type=pl.DeviceIdType.MESH,
        )

    outs = ((audio_mixed, audio_out, arows), (video_mixed, video_out, rows))

    def own_out(kind):
        source, target, count = outs[kind]
        return pltpu.make_async_copy(
            source.at[token_rows(me, count), :],
            target.at[:, head_columns(me)],
            out_own_sem.at[kind],
        )

    def sent_out(kind, peer):
        source, target, count = outs[kind]
        return pltpu.make_async_remote_copy(
            src_ref=source.at[token_rows(peer, count), :],
            dst_ref=target.at[:, head_columns(me)],
            send_sem=out_send_sem.at[kind, peer],
            recv_sem=out_recv_sem.at[kind, me],
            device_id={"seq": peer},
            device_id_type=pl.DeviceIdType.MESH,
        )

    def received_out(kind, peer):
        source, target, count = outs[kind]
        return pltpu.make_async_remote_copy(
            src_ref=source.at[token_rows(peer, count), :],
            dst_ref=target.at[:, head_columns(peer)],
            send_sem=out_send_sem.at[kind, peer],
            recv_sem=out_recv_sem.at[kind, peer],
            device_id={"seq": peer},
            device_id_type=pl.DeviceIdType.MESH,
        )

    for kind in range(len(ins)):
        own_in(kind).start()

    def signal(semaphore, peer):
        pl.semaphore_signal(
            semaphore,
            inc=1,
            device_id={"seq": peer},
            device_id_type=pl.DeviceIdType.MESH,
        )

    def send(kinds, peers):
        for kind in kinds:
            for peer in peers:
                sent_in(kind, peer).start()

    barrier = pltpu.get_barrier_semaphore()
    near = [near_peer(step, 1) for step in range(1, half)]
    far = [far_peer(step, 1) for step in range(far_count)]
    for peer in far[:1] + near:
        signal(barrier, peer)
    pl.semaphore_wait(barrier, len(far[:1] + near))
    for peer in near:
        signal(far_in_sem, peer)
    for kinds, which in EARLY_ORDER:
        send(kinds, near if which == "near" else far[:1])
    if near:
        pl.semaphore_wait(far_in_sem, len(near))
    for kinds, which in LATE_ORDER:
        send(kinds, {"near": near, "rest": far[1:], "far": far}[which])

    ones = jnp.ones((arows * n, HEAD_DIM), jnp.bfloat16)
    av[:, HEAD_DIM:] = ones
    audio_self[:, HEAD_DIM:] = ones
    ones = jnp.ones((rows * n, HEAD_DIM), jnp.bfloat16)
    vv[:, HEAD_DIM:] = ones
    audio_sum[...] = jnp.zeros_like(audio_sum)

    def wait_kinds(kinds):
        for kind in kinds:
            own_in(kind).wait()

        def wait_peer(peer):
            for kind in kinds:
                received_in(kind, peer).wait_recv()

        over_peers(wait_peer, -1, False)

    def dot_t(left, right):
        return lax.dot_general(
            left, right, (((1,), (1,)), ((), ())), preferred_element_type=jnp.float32
        )

    def dot(left, right):
        return jnp.dot(left, right, preferred_element_type=jnp.float32)

    def self_attend(queries, key_rows, values):
        scores = dot_t(queries, key_rows)
        largest = jnp.max(scores, axis=1, keepdims=True)
        weights = jnp.exp2((scores - largest) * EXP2_SCALE).astype(jnp.bfloat16)
        both = dot(weights, values)
        return (both[:, :HEAD_DIM] / both[:, HEAD_DIM:]).astype(jnp.bfloat16)

    def unit(tokens):
        entries = tokens.astype(jnp.float32)
        mean = jnp.mean(entries * entries, axis=1, keepdims=True)
        return entries * lax.rsqrt(mean + 1e-06)

    own_head = pl.ds(me, 1)
    wait_kinds((0, 1, 2))
    tokens = self_attend(aq[...], ak[...], av[...])
    audio_self[:, :HEAD_DIM] = tokens
    scaled = unit(tokens)
    audio_queries[...] = (scaled * audio_query_gain[own_head, :]).astype(jnp.bfloat16)
    audio_keys[...] = (scaled * audio_key_gain[own_head, :]).astype(jnp.bfloat16)

    wait_kinds((3, 4))

    def self_part(peers):
        here = [token_rows(peer, rows) for peer in peers]
        tokens = self_attend(jnp.concatenate([vq[one, :] for one in here], 0), vk[...], vv[...])
        scaled = unit(tokens)
        queries = (scaled * video_query_gain[own_head, :]).astype(jnp.bfloat16)
        key_rows = (scaled * video_key_gain[own_head, :]).astype(jnp.bfloat16)
        return tokens, queries, key_rows

    def audio_part(tokens, key_rows):
        weights = jnp.exp2(dot_t(audio_queries[...], key_rows) * EXP2_SCALE)
        values = jnp.concatenate([tokens, jnp.ones_like(tokens)], 1)
        audio_sum[...] += dot(weights.astype(jnp.bfloat16), values)

    def video_part(peers, tokens, queries):
        weights = jnp.exp2(dot_t(queries, audio_keys[...]) * EXP2_SCALE)
        both = dot(weights.astype(jnp.bfloat16), audio_self[...])
        cross = both[:, :HEAD_DIM] / both[:, HEAD_DIM:]
        mixed = (tokens.astype(jnp.float32) + cross).astype(jnp.bfloat16)
        for index, peer in enumerate(peers):
            video_mixed[token_rows(peer, rows), :] = mixed[index * rows : (index + 1) * rows]

    def send_audio(peer):
        sent_out(0, peer).start()

    others = [far_peer(step, -1) for step in range(far_count)]
    others += [near_peer(step, -1) for step in range(1, half)]
    group = GROUP if n % GROUP == 0 else 1
    for first in range(0, n, group):
        last = first + group == n
        here = others[first : first + group]
        for peer in here:
            received_in(5, peer).wait_recv()
        if last:
            own_in(5).wait()
        peers = here + [me] if last else here
        tokens, queries, key_rows = self_part(peers)
        if not last:
            video_part(peers, tokens, queries)
            for peer in here:
                sent_out(1, peer).start()
            audio_part(tokens, key_rows)
        else:
            audio_part(tokens, key_rows)
            both = audio_sum[...]
            cross = both[:, :HEAD_DIM] / both[:, HEAD_DIM:]
            audio_mixed[...] = (
                audio_self[:, :HEAD_DIM].astype(jnp.float32) + cross
            ).astype(jnp.bfloat16)
            own_out(0).start()
            over_peers(send_audio, 1, True)
            video_part(peers, tokens, queries)
            for peer in here:
                sent_out(1, peer).start()
            own_out(1).start()

    def finish_peer(peer):
        for kind in range(len(ins)):
            sent_in(kind, peer).wait_send()
        for kind in range(len(outs)):
            sent_out(kind, peer).wait_send()
            received_out(kind, peer).wait_recv()

    over_peers(finish_peer, 1, True)
    own_out(0).wait()
    own_out(1).wait()


def pass_on_kernel(
    video_in, audio_in, video_out, audio_out, video_held, audio_held, in_sem, out_sem
):
    loads, stores = [], []
    for kind, (source, held, target) in enumerate(
        ((video_in, video_held, video_out), (audio_in, audio_held, audio_out))
    ):
        piece = source.shape[1] // PIECES
        for index in range(PIECES):
            here = (slice(None), pl.ds(index * piece, piece))
            loads.append(
                pltpu.make_async_copy(source.at[here], held.at[here], in_sem.at[kind, index])
            )
            stores.append(
                pltpu.make_async_copy(held.at[here], target.at[here], out_sem.at[kind, index])
            )
    for load in loads:
        load.start()
    for load, store in zip(loads, stores):
        load.wait()
        store.start()
    for store in stores:
        store.wait()


PIECES = 2
GROUP = 2
EARLY_ORDER = (((0, 1, 2), "first"), ((0, 1, 2), "near"), ((3, 4), "first"), ((3, 4), "near"))
LATE_ORDER = (((0, 1, 2), "rest"), ((3, 4), "rest"), ((5,), "far"), ((5,), "near"))


def head_per_device(n, *arrays):
    video_q, audio_q = arrays[0], arrays[3]
    tokens, atokens = video_q.shape[0] * n, audio_q.shape[0] * n
    bf16, f32 = jnp.bfloat16, jnp.float32
    gains = [gain.reshape(n, HEAD_DIM) for gain in arrays[6:]]
    anywhere = pl.BlockSpec(memory_space=pl.ANY)
    vmem = pl.BlockSpec(memory_space=pltpu.VMEM)
    results = pl.pallas_call(
        functools.partial(attend_kernel, n),
        out_shape=(
            jax.ShapeDtypeStruct(video_q.shape, bf16),
            jax.ShapeDtypeStruct(audio_q.shape, bf16),
        ),
        in_specs=[anywhere] * 6 + [vmem] * 4,
        out_specs=(anywhere, anywhere),
        scratch_shapes=[
            pltpu.VMEM((tokens, HEAD_DIM), bf16),
            pltpu.VMEM((tokens, HEAD_DIM), bf16),
            pltpu.VMEM((tokens, 2 * HEAD_DIM), bf16),
            pltpu.VMEM((atokens, HEAD_DIM), bf16),
            pltpu.VMEM((atokens, HEAD_DIM), bf16),
            pltpu.VMEM((atokens, 2 * HEAD_DIM), bf16),
            pltpu.VMEM((atokens, 2 * HEAD_DIM), bf16),
            pltpu.VMEM((atokens, HEAD_DIM), bf16),
            pltpu.VMEM((atokens, HEAD_DIM), bf16),
            pltpu.VMEM((atokens, 2 * HEAD_DIM), f32),
            pltpu.VMEM((tokens, HEAD_DIM), bf16),
            pltpu.VMEM((atokens, HEAD_DIM), bf16),
            pltpu.SemaphoreType.DMA((6, n)),
            pltpu.SemaphoreType.DMA((6, n)),
            pltpu.SemaphoreType.DMA((6,)),
            pltpu.SemaphoreType.DMA((2, n)),
            pltpu.SemaphoreType.DMA((2, n)),
            pltpu.SemaphoreType.DMA((2,)),
            pltpu.SemaphoreType.REGULAR,
        ],
        compiler_params=pltpu.CompilerParams(collective_id=0, has_side_effects=True),
    )(*arrays[:6], *gains)
    return pl.pallas_call(
        pass_on_kernel,
        out_shape=(
            jax.ShapeDtypeStruct(video_q.shape, bf16),
            jax.ShapeDtypeStruct(audio_q.shape, bf16),
        ),
        in_specs=[anywhere] * 2,
        out_specs=(anywhere, anywhere),
        scratch_shapes=[
            pltpu.VMEM(video_q.shape, bf16),
            pltpu.VMEM(audio_q.shape, bf16),
            pltpu.SemaphoreType.DMA((2, PIECES)),
            pltpu.SemaphoreType.DMA((2, PIECES)),
        ],
    )(*results)


def solution(mesh):
    in_specs = (
        P(("clips", "seq"), "head"),
        P(("clips", "seq"), "head"),
        P(("clips", "seq"), "head"),
        P(("clips", "seq"), "head"),
        P(("clips", "seq"), "head"),
        P(("clips", "seq"), "head"),
        P("head"),
        P("head"),
        P("head"),
        P("head"),
    )
    out_specs = (P(("clips", "seq"), "head"), P(("clips", "seq"), "head"))
    sizes = dict(mesh.shape)

    def body(*arrays):
        video_q, audio_q = arrays[0], arrays[3]
        if (
            video_q.shape[1] == sizes["seq"] * HEAD_DIM
            and video_q.shape[0] % 16 == 0
            and audio_q.shape[0] % 16 == 0
        ):
            return head_per_device(sizes["seq"], *arrays)
        return per_device(*arrays)

    return jax.shard_map(
        body, mesh=mesh, in_specs=in_specs, out_specs=out_specs, check_vma=False
    )
```

```python
import functools
import math

import jax
import jax.numpy as jnp
from jax import lax
from jax.experimental import pallas as pl
from jax.experimental.pallas import tpu as pltpu
from jax.sharding import PartitionSpec as P

HEAD_DIM = 128
EXP2_SCALE = HEAD_DIM ** (-0.5) * math.log2(math.e)


def normed(tokens, gain_row):
    count = tokens.shape[0]
    head_count = tokens.shape[1] // HEAD_DIM
    entries = tokens.astype(jnp.float32).reshape(count, head_count, HEAD_DIM)
    scaled = entries * lax.rsqrt(jnp.mean(entries * entries, axis=2, keepdims=True) + 1e-06)
    return (scaled.reshape(count, head_count * HEAD_DIM) * gain_row).astype(jnp.bfloat16)


def start_state(row_count, head_count):
    return (
        jnp.full((head_count, row_count), -1e30, jnp.float32),
        jnp.zeros((head_count, row_count), jnp.float32),
        jnp.zeros((row_count, head_count, HEAD_DIM), jnp.float32),
    )


def folding(queries, prepare):
    head_count = queries.shape[1]

    def fold_step(state_now, pieces, offset):
        key_rows, values = prepare(pieces)
        key_rows = key_rows.reshape(key_rows.shape[0], head_count, HEAD_DIM)
        values = values.reshape(values.shape[0], head_count, HEAD_DIM)
        scores = jnp.einsum(
            "qhd,khd->hqk", queries, key_rows, preferred_element_type=jnp.float32
        ) * HEAD_DIM ** (-0.5)
        running_max, row_total, accumulated = state_now
        new_max = jnp.maximum(running_max, jnp.max(scores, axis=2))
        rescale = jnp.exp(running_max - new_max)
        weights = jnp.exp(scores - new_max[:, :, None])
        row_total = jnp.sum(weights, axis=2)
        update = jnp.einsum(
            "hqk,khd->qhd", weights.astype(jnp.bfloat16), values, preferred_element_type=jnp.float32
        )
        accumulated = accumulated * rescale.T[:, :, None] + update
        return (new_max, row_total, accumulated)

    return fold_step


def finish(state_now):
    running_max, row_total, accumulated = state_now
    result = accumulated / row_total.T[:, :, None]
    return result.reshape(result.shape[0], result.shape[1] * HEAD_DIM)


def as_heads(tokens):
    return tokens.reshape(tokens.shape[0], tokens.shape[1] // HEAD_DIM, HEAD_DIM)


def keep_pair(pieces):
    return pieces


def per_device(
    video_q,
    video_k,
    video_v,
    audio_q,
    audio_k,
    audio_v,
    video_query_gain,
    video_key_gain,
    audio_query_gain,
    audio_key_gain,
):
    head_count = video_q.shape[1] // HEAD_DIM
    video_rows = video_q.shape[0]
    audio_rows = audio_q.shape[0]
    video_state = folding(as_heads(video_q), keep_pair)(
        start_state(video_rows, head_count),
        (
            lax.all_gather(video_k, "seq", axis=0, tiled=True),
            lax.all_gather(video_v, "seq", axis=0, tiled=True),
        ),
        jnp.int32(0),
    )
    video_self = finish(video_state).astype(jnp.bfloat16)
    audio_state = folding(as_heads(audio_q), keep_pair)(
        start_state(audio_rows, head_count),
        (
            lax.all_gather(audio_k, "seq", axis=0, tiled=True),
            lax.all_gather(audio_v, "seq", axis=0, tiled=True),
        ),
        jnp.int32(0),
    )
    audio_self = finish(audio_state).astype(jnp.bfloat16)
    audio_whole = lax.all_gather(audio_self, "seq", axis=0, tiled=True)
    video_queries = as_heads(normed(video_self, video_query_gain))
    cross_step = folding(video_queries, keep_pair)
    video_cross = finish(
        cross_step(
            start_state(video_rows, head_count),
            (normed(audio_whole, audio_key_gain), audio_whole),
            0,
        )
    )
    audio_queries = normed(audio_self, audio_query_gain)

    def prepare_video(shard_rows):
        return (normed(shard_rows, video_key_gain), shard_rows)

    audio_state_cross = folding(as_heads(audio_queries), prepare_video)(
        start_state(audio_rows, head_count),
        lax.all_gather(video_self, "seq", axis=0, tiled=True),
        jnp.int32(0),
    )
    audio_cross = finish(audio_state_cross)
    video_mixed = (video_self.astype(jnp.float32) + video_cross).astype(jnp.bfloat16)
    audio_mixed = (audio_self.astype(jnp.float32) + audio_cross).astype(jnp.bfloat16)
    return (video_mixed, audio_mixed)


def attend_kernel(
    n,
    video_q,
    video_k,
    video_v,
    audio_q,
    audio_k,
    audio_v,
    video_query_gain_in,
    video_key_gain_in,
    audio_query_gain_in,
    audio_key_gain_in,
    video_out,
    audio_out,
    vq,
    vk,
    vv,
    aq,
    ak,
    av,
    audio_self,
    audio_queries,
    audio_keys,
    audio_sum,
    video_mixed,
    audio_mixed,
    send_sem,
    recv_sem,
    own_sem,
    out_send_sem,
    out_recv_sem,
    out_own_sem,
    far_in_sem,
    video_query_gain,
    video_key_gain,
    audio_query_gain,
    audio_key_gain,
    gain_sem,
):
    me = lax.axis_index("seq")
    rows = video_q.shape[0]
    arows = audio_q.shape[0]

    half = n // 2 if n % 2 == 0 else n
    far_count = n - half

    def near_peer(step, sign):
        return me // half * half + lax.rem(lax.rem(me, half) + half + sign * step, half)

    def far_peer(step, sign):
        return lax.rem(near_peer(step, sign) + half, n)

    def over_peers(visit, sign, far_first):
        def far(step, carry):
            visit(far_peer(step, sign))
            return carry

        def near(step, carry):
            visit(near_peer(step, sign))
            return carry

        if far_first:
            lax.fori_loop(0, far_count, far, 0)
        lax.fori_loop(1, half, near, 0)
        if not far_first:
            lax.fori_loop(0, far_count, far, 0)

    def head_columns(index):
        return pl.ds(pl.multiple_of(index * HEAD_DIM, HEAD_DIM), HEAD_DIM)

    def token_rows(index, count):
        return pl.ds(pl.multiple_of(index * count, count), count)

    ins = (
        (audio_k, ak, arows),
        (audio_v, av, arows),
        (audio_q, aq, arows),
        (video_k, vk, rows),
        (video_v, vv, rows),
        (video_q, vq, rows),
    )

    def own_in(kind):
        source, target, count = ins[kind]
        return pltpu.make_async_copy(
            source.at[:, head_columns(me)],
            target.at[token_rows(me, count), pl.ds(0, HEAD_DIM)],
            own_sem.at[kind],
        )

    def sent_in(kind, peer):
        source, target, count = ins[kind]
        return pltpu.make_async_remote_copy(
            src_ref=source.at[:, head_columns(peer)],
            dst_ref=target.at[token_rows(me, count), pl.ds(0, HEAD_DIM)],
            send_sem=send_sem.at[kind, peer],
            recv_sem=recv_sem.at[kind, me],
            device_id={"seq": peer},
            device_id_type=pl.DeviceIdType.MESH,
        )

    def received_in(kind, peer):
        source, target, count = ins[kind]
        return pltpu.make_async_remote_copy(
            src_ref=source.at[:, head_columns(peer)],
            dst_ref=target.at[token_rows(peer, count), pl.ds(0, HEAD_DIM)],
            send_sem=send_sem.at[kind, peer],
            recv_sem=recv_sem.at[kind, peer],
            device_id={"seq": peer},
            device_id_type=pl.DeviceIdType.MESH,
        )

    outs = ((audio_mixed, audio_out, arows), (video_mixed, video_out, rows))

    def own_out(kind):
        source, target, count = outs[kind]
        return pltpu.make_async_copy(
            source.at[token_rows(me, count), :],
            target.at[:, head_columns(me)],
            out_own_sem.at[kind],
        )

    def sent_out(kind, peer):
        source, target, count = outs[kind]
        return pltpu.make_async_remote_copy(
            src_ref=source.at[token_rows(peer, count), :],
            dst_ref=target.at[:, head_columns(me)],
            send_sem=out_send_sem.at[kind, peer],
            recv_sem=out_recv_sem.at[kind, me],
            device_id={"seq": peer},
            device_id_type=pl.DeviceIdType.MESH,
        )

    def received_out(kind, peer):
        source, target, count = outs[kind]
        return pltpu.make_async_remote_copy(
            src_ref=source.at[token_rows(peer, count), :],
            dst_ref=target.at[:, head_columns(peer)],
            send_sem=out_send_sem.at[kind, peer],
            recv_sem=out_recv_sem.at[kind, peer],
            device_id={"seq": peer},
            device_id_type=pl.DeviceIdType.MESH,
        )

    def signal(semaphore, peer):
        pl.semaphore_signal(
            semaphore,
            inc=1,
            device_id={"seq": peer},
            device_id_type=pl.DeviceIdType.MESH,
        )

    def send(kinds, peers):
        for kind in kinds:
            for peer in peers:
                sent_in(kind, peer).start()

    barrier = pltpu.get_barrier_semaphore()
    near = [near_peer(step, 1) for step in range(1, half)]
    far = [far_peer(step, 1) for step in range(far_count)]
    for peer in far[:1] + near:
        signal(barrier, peer)
    pl.semaphore_wait(barrier, len(far[:1] + near))
    for peer in near:
        signal(far_in_sem, peer)
    for kinds, which in EARLY_ORDER:
        send(kinds, near if which == "near" else far[:1])
    if near:
        pl.semaphore_wait(far_in_sem, len(near))
    for kinds, which in LATE_ORDER:
        send(kinds, {"near": near, "rest": far[1:], "far": far}[which])

    gains = [
        pltpu.make_async_copy(source, target, gain_sem.at[index])
        for index, (source, target) in enumerate(
            (
                (video_query_gain_in, video_query_gain),
                (video_key_gain_in, video_key_gain),
                (audio_query_gain_in, audio_query_gain),
                (audio_key_gain_in, audio_key_gain),
            )
        )
    ]
    for gain in gains:
        gain.start()
    for kind in range(len(ins)):
        own_in(kind).start()

    ones = jnp.ones((arows * n, HEAD_DIM), jnp.bfloat16)
    av[:, HEAD_DIM:] = ones
    audio_self[:, HEAD_DIM:] = ones
    ones = jnp.ones((rows * n, HEAD_DIM), jnp.bfloat16)
    vv[:, HEAD_DIM:] = ones
    audio_sum[...] = jnp.zeros_like(audio_sum)

    def wait_kinds(kinds):
        for kind in kinds:
            own_in(kind).wait()

        def wait_peer(peer):
            for kind in kinds:
                received_in(kind, peer).wait_recv()

        over_peers(wait_peer, -1, False)

    def dot_t(left, right):
        return lax.dot_general(
            left, right, (((1,), (1,)), ((), ())), preferred_element_type=jnp.float32
        )

    def dot(left, right):
        return jnp.dot(left, right, preferred_element_type=jnp.float32)

    def self_attend(queries, key_rows, values):
        scores = dot_t(queries, key_rows)
        largest = jnp.max(scores, axis=1, keepdims=True)
        weights = jnp.exp2((scores - largest) * EXP2_SCALE).astype(jnp.bfloat16)
        both = dot(weights, values)
        return (both[:, :HEAD_DIM] / both[:, HEAD_DIM:]).astype(jnp.bfloat16)

    def unit(tokens):
        entries = tokens.astype(jnp.float32)
        mean = jnp.mean(entries * entries, axis=1, keepdims=True)
        return entries * lax.rsqrt(mean + 1e-06)

    own_head = pl.ds(me, 1)
    for gain in gains:
        gain.wait()
    wait_kinds((0, 1, 2))
    tokens = self_attend(aq[...], ak[...], av[...])
    audio_self[:, :HEAD_DIM] = tokens
    scaled = unit(tokens)
    audio_queries[...] = (scaled * audio_query_gain[own_head, :]).astype(jnp.bfloat16)
    audio_keys[...] = (scaled * audio_key_gain[own_head, :]).astype(jnp.bfloat16)

    wait_kinds((3, 4))

    def self_part(peers):
        here = [token_rows(peer, rows) for peer in peers]
        tokens = self_attend(jnp.concatenate([vq[one, :] for one in here], 0), vk[...], vv[...])
        scaled = unit(tokens)
        queries = (scaled * video_query_gain[own_head, :]).astype(jnp.bfloat16)
        key_rows = (scaled * video_key_gain[own_head, :]).astype(jnp.bfloat16)
        return tokens, queries, key_rows

    def audio_part(tokens, key_rows):
        weights = jnp.exp2(dot_t(audio_queries[...], key_rows) * EXP2_SCALE)
        values = jnp.concatenate([tokens, jnp.ones_like(tokens)], 1)
        audio_sum[...] += dot(weights.astype(jnp.bfloat16), values)

    def video_part(peers, tokens, queries):
        weights = jnp.exp2(dot_t(queries, audio_keys[...]) * EXP2_SCALE)
        both = dot(weights.astype(jnp.bfloat16), audio_self[...])
        cross = both[:, :HEAD_DIM] / both[:, HEAD_DIM:]
        mixed = (tokens.astype(jnp.float32) + cross).astype(jnp.bfloat16)
        for index, peer in enumerate(peers):
            video_mixed[token_rows(peer, rows), :] = mixed[index * rows : (index + 1) * rows]

    def send_audio(peer):
        sent_out(0, peer).start()

    others = [far_peer(step, -1) for step in range(far_count)]
    others += [near_peer(step, -1) for step in range(1, half)]
    group = GROUP if n % GROUP == 0 else 1
    for first in range(0, n, group):
        last = first + group == n
        here = others[first : first + group]
        for peer in here:
            received_in(5, peer).wait_recv()
        if last:
            own_in(5).wait()
        peers = here + [me] if last else here
        tokens, queries, key_rows = self_part(peers)
        if not last:
            video_part(peers, tokens, queries)
            for peer in here:
                sent_out(1, peer).start()
            audio_part(tokens, key_rows)
        else:
            audio_part(tokens, key_rows)
            both = audio_sum[...]
            cross = both[:, :HEAD_DIM] / both[:, HEAD_DIM:]
            audio_mixed[...] = (
                audio_self[:, :HEAD_DIM].astype(jnp.float32) + cross
            ).astype(jnp.bfloat16)
            own_out(0).start()
            over_peers(send_audio, 1, True)
            video_part(peers, tokens, queries)
            for peer in here:
                sent_out(1, peer).start()
            own_out(1).start()

    def finish_peer(peer):
        for kind in range(len(ins)):
            sent_in(kind, peer).wait_send()
        for kind in range(len(outs)):
            sent_out(kind, peer).wait_send()
            received_out(kind, peer).wait_recv()

    over_peers(finish_peer, 1, True)
    own_out(0).wait()
    own_out(1).wait()


def pass_on_kernel(video_in, audio_in, video_out, audio_out, sem):
    copies = (
        pltpu.make_async_copy(video_in, video_out, sem.at[0]),
        pltpu.make_async_copy(audio_in, audio_out, sem.at[1]),
    )
    for copy in copies:
        copy.start()
    for copy in copies:
        copy.wait()


GROUP = 2
KERNEL_BYTES = 24 * 2**20
EARLY_ORDER = (((0, 1, 2), "first"), ((0, 1, 2), "near"), ((3, 4), "first"), ((3, 4), "near"))
LATE_ORDER = (((0, 1, 2), "rest"), ((3, 4), "rest"), ((5,), "far"), ((5,), "near"))


def head_per_device(n, *arrays):
    video_q, audio_q = arrays[0], arrays[3]
    tokens, atokens = video_q.shape[0] * n, audio_q.shape[0] * n
    bf16, f32 = jnp.bfloat16, jnp.float32
    gains = [gain.reshape(n, HEAD_DIM) for gain in arrays[6:]]
    anywhere = pl.BlockSpec(memory_space=pl.ANY)
    operands = [
        pltpu.with_memory_space_constraint(one, pltpu.HBM) for one in (*arrays[:6], *gains)
    ]
    results = pl.pallas_call(
        functools.partial(attend_kernel, n),
        out_shape=(
            jax.ShapeDtypeStruct(video_q.shape, bf16),
            jax.ShapeDtypeStruct(audio_q.shape, bf16),
        ),
        in_specs=[anywhere] * 10,
        out_specs=(anywhere, anywhere),
        scratch_shapes=[
            pltpu.VMEM((tokens, HEAD_DIM), bf16),
            pltpu.VMEM((tokens, HEAD_DIM), bf16),
            pltpu.VMEM((tokens, 2 * HEAD_DIM), bf16),
            pltpu.VMEM((atokens, HEAD_DIM), bf16),
            pltpu.VMEM((atokens, HEAD_DIM), bf16),
            pltpu.VMEM((atokens, 2 * HEAD_DIM), bf16),
            pltpu.VMEM((atokens, 2 * HEAD_DIM), bf16),
            pltpu.VMEM((atokens, HEAD_DIM), bf16),
            pltpu.VMEM((atokens, HEAD_DIM), bf16),
            pltpu.VMEM((atokens, 2 * HEAD_DIM), f32),
            pltpu.VMEM((tokens, HEAD_DIM), bf16),
            pltpu.VMEM((atokens, HEAD_DIM), bf16),
            pltpu.SemaphoreType.DMA((6, n)),
            pltpu.SemaphoreType.DMA((6, n)),
            pltpu.SemaphoreType.DMA((6,)),
            pltpu.SemaphoreType.DMA((2, n)),
            pltpu.SemaphoreType.DMA((2, n)),
            pltpu.SemaphoreType.DMA((2,)),
            pltpu.SemaphoreType.REGULAR,
            *[pltpu.VMEM((n, HEAD_DIM), f32)] * 4,
            pltpu.SemaphoreType.DMA((4,)),
        ],
        compiler_params=pltpu.CompilerParams(
            collective_id=0, has_side_effects=True, vmem_limit_bytes=KERNEL_BYTES
        ),
    )(*operands)
    return pl.pallas_call(
        pass_on_kernel,
        out_shape=(
            jax.ShapeDtypeStruct(video_q.shape, bf16),
            jax.ShapeDtypeStruct(audio_q.shape, bf16),
        ),
        in_specs=[anywhere] * 2,
        out_specs=(anywhere, anywhere),
        scratch_shapes=[pltpu.SemaphoreType.DMA((2,))],
        compiler_params=pltpu.CompilerParams(vmem_limit_bytes=KERNEL_BYTES // 4),
    )(*results)


def solution(mesh):
    in_specs = (
        P(("clips", "seq"), "head"),
        P(("clips", "seq"), "head"),
        P(("clips", "seq"), "head"),
        P(("clips", "seq"), "head"),
        P(("clips", "seq"), "head"),
        P(("clips", "seq"), "head"),
        P("head"),
        P("head"),
        P("head"),
        P("head"),
    )
    out_specs = (P(("clips", "seq"), "head"), P(("clips", "seq"), "head"))
    sizes = dict(mesh.shape)

    def body(*arrays):
        video_q, audio_q = arrays[0], arrays[3]
        if (
            video_q.shape[1] == sizes["seq"] * HEAD_DIM
            and video_q.shape[0] % 16 == 0
            and audio_q.shape[0] % 16 == 0
        ):
            return head_per_device(sizes["seq"], *arrays)
        return per_device(*arrays)

    return jax.shard_map(
        body, mesh=mesh, in_specs=in_specs, out_specs=out_specs, check_vma=False
    )
```

```python
import functools
import math

import jax
import jax.numpy as jnp
from jax import lax
from jax.experimental import pallas as pl
from jax.experimental.pallas import tpu as pltpu
from jax.sharding import PartitionSpec as P

HEAD_DIM = 128
EXP2_SCALE = HEAD_DIM ** (-0.5) * math.log2(math.e)


def normed(tokens, gain_row):
    count = tokens.shape[0]
    head_count = tokens.shape[1] // HEAD_DIM
    entries = tokens.astype(jnp.float32).reshape(count, head_count, HEAD_DIM)
    scaled = entries * lax.rsqrt(jnp.mean(entries * entries, axis=2, keepdims=True) + 1e-06)
    return (scaled.reshape(count, head_count * HEAD_DIM) * gain_row).astype(jnp.bfloat16)


def start_state(row_count, head_count):
    return (
        jnp.full((head_count, row_count), -1e30, jnp.float32),
        jnp.zeros((head_count, row_count), jnp.float32),
        jnp.zeros((row_count, head_count, HEAD_DIM), jnp.float32),
    )


def folding(queries, prepare):
    head_count = queries.shape[1]

    def fold_step(state_now, pieces, offset):
        key_rows, values = prepare(pieces)
        key_rows = key_rows.reshape(key_rows.shape[0], head_count, HEAD_DIM)
        values = values.reshape(values.shape[0], head_count, HEAD_DIM)
        scores = jnp.einsum(
            "qhd,khd->hqk", queries, key_rows, preferred_element_type=jnp.float32
        ) * HEAD_DIM ** (-0.5)
        running_max, row_total, accumulated = state_now
        new_max = jnp.maximum(running_max, jnp.max(scores, axis=2))
        rescale = jnp.exp(running_max - new_max)
        weights = jnp.exp(scores - new_max[:, :, None])
        row_total = jnp.sum(weights, axis=2)
        update = jnp.einsum(
            "hqk,khd->qhd", weights.astype(jnp.bfloat16), values, preferred_element_type=jnp.float32
        )
        accumulated = accumulated * rescale.T[:, :, None] + update
        return (new_max, row_total, accumulated)

    return fold_step


def finish(state_now):
    running_max, row_total, accumulated = state_now
    result = accumulated / row_total.T[:, :, None]
    return result.reshape(result.shape[0], result.shape[1] * HEAD_DIM)


def as_heads(tokens):
    return tokens.reshape(tokens.shape[0], tokens.shape[1] // HEAD_DIM, HEAD_DIM)


def keep_pair(pieces):
    return pieces


def per_device(
    video_q,
    video_k,
    video_v,
    audio_q,
    audio_k,
    audio_v,
    video_query_gain,
    video_key_gain,
    audio_query_gain,
    audio_key_gain,
):
    head_count = video_q.shape[1] // HEAD_DIM
    video_rows = video_q.shape[0]
    audio_rows = audio_q.shape[0]
    video_state = folding(as_heads(video_q), keep_pair)(
        start_state(video_rows, head_count),
        (
            lax.all_gather(video_k, "seq", axis=0, tiled=True),
            lax.all_gather(video_v, "seq", axis=0, tiled=True),
        ),
        jnp.int32(0),
    )
    video_self = finish(video_state).astype(jnp.bfloat16)
    audio_state = folding(as_heads(audio_q), keep_pair)(
        start_state(audio_rows, head_count),
        (
            lax.all_gather(audio_k, "seq", axis=0, tiled=True),
            lax.all_gather(audio_v, "seq", axis=0, tiled=True),
        ),
        jnp.int32(0),
    )
    audio_self = finish(audio_state).astype(jnp.bfloat16)
    audio_whole = lax.all_gather(audio_self, "seq", axis=0, tiled=True)
    video_queries = as_heads(normed(video_self, video_query_gain))
    cross_step = folding(video_queries, keep_pair)
    video_cross = finish(
        cross_step(
            start_state(video_rows, head_count),
            (normed(audio_whole, audio_key_gain), audio_whole),
            0,
        )
    )
    audio_queries = normed(audio_self, audio_query_gain)

    def prepare_video(shard_rows):
        return (normed(shard_rows, video_key_gain), shard_rows)

    audio_state_cross = folding(as_heads(audio_queries), prepare_video)(
        start_state(audio_rows, head_count),
        lax.all_gather(video_self, "seq", axis=0, tiled=True),
        jnp.int32(0),
    )
    audio_cross = finish(audio_state_cross)
    video_mixed = (video_self.astype(jnp.float32) + video_cross).astype(jnp.bfloat16)
    audio_mixed = (audio_self.astype(jnp.float32) + audio_cross).astype(jnp.bfloat16)
    return (video_mixed, audio_mixed)


def attend_kernel(
    n,
    video_q,
    video_k,
    video_v,
    audio_q,
    audio_k,
    audio_v,
    video_query_gain_in,
    video_key_gain_in,
    audio_query_gain_in,
    audio_key_gain_in,
    video_out,
    audio_out,
    vq,
    vk,
    vv,
    aq,
    ak,
    av,
    audio_self,
    audio_queries,
    audio_keys,
    audio_sum,
    video_mixed,
    audio_mixed,
    send_sem,
    recv_sem,
    own_sem,
    out_send_sem,
    out_recv_sem,
    out_own_sem,
    far_in_sem,
    video_query_gain,
    video_key_gain,
    audio_query_gain,
    audio_key_gain,
    gain_sem,
):
    me = lax.axis_index("seq")
    rows = video_q.shape[0]
    arows = audio_q.shape[0]

    half = n // 2 if n % 2 == 0 else n
    far_count = n - half

    def near_peer(step, sign):
        return me // half * half + lax.rem(lax.rem(me, half) + half + sign * step, half)

    def far_peer(step, sign):
        return lax.rem(near_peer(step, sign) + half, n)

    def over_peers(visit, sign, far_first):
        def far(step, carry):
            visit(far_peer(step, sign))
            return carry

        def near(step, carry):
            visit(near_peer(step, sign))
            return carry

        if far_first:
            lax.fori_loop(0, far_count, far, 0)
        lax.fori_loop(1, half, near, 0)
        if not far_first:
            lax.fori_loop(0, far_count, far, 0)

    def head_columns(index):
        return pl.ds(pl.multiple_of(index * HEAD_DIM, HEAD_DIM), HEAD_DIM)

    def token_rows(index, count):
        return pl.ds(pl.multiple_of(index * count, count), count)

    ins = (
        (audio_k, ak, arows),
        (audio_v, av, arows),
        (audio_q, aq, arows),
        (video_k, vk, rows),
        (video_v, vv, rows),
        (video_q, vq, rows),
    )

    def own_in(kind):
        source, target, count = ins[kind]
        return pltpu.make_async_copy(
            source.at[:, head_columns(me)],
            target.at[token_rows(me, count), pl.ds(0, HEAD_DIM)],
            own_sem.at[kind],
        )

    def sent_in(kind, peer):
        source, target, count = ins[kind]
        return pltpu.make_async_remote_copy(
            src_ref=source.at[:, head_columns(peer)],
            dst_ref=target.at[token_rows(me, count), pl.ds(0, HEAD_DIM)],
            send_sem=send_sem.at[kind, peer],
            recv_sem=recv_sem.at[kind, me],
            device_id={"seq": peer},
            device_id_type=pl.DeviceIdType.MESH,
        )

    def received_in(kind, peer):
        source, target, count = ins[kind]
        return pltpu.make_async_remote_copy(
            src_ref=source.at[:, head_columns(peer)],
            dst_ref=target.at[token_rows(peer, count), pl.ds(0, HEAD_DIM)],
            send_sem=send_sem.at[kind, peer],
            recv_sem=recv_sem.at[kind, peer],
            device_id={"seq": peer},
            device_id_type=pl.DeviceIdType.MESH,
        )

    outs = ((audio_mixed, audio_out, arows), (video_mixed, video_out, rows))

    def own_out(kind):
        source, target, count = outs[kind]
        return pltpu.make_async_copy(
            source.at[token_rows(me, count), :],
            target.at[:, head_columns(me)],
            out_own_sem.at[kind],
        )

    def sent_out(kind, peer):
        source, target, count = outs[kind]
        return pltpu.make_async_remote_copy(
            src_ref=source.at[token_rows(peer, count), :],
            dst_ref=target.at[:, head_columns(me)],
            send_sem=out_send_sem.at[kind, peer],
            recv_sem=out_recv_sem.at[kind, me],
            device_id={"seq": peer},
            device_id_type=pl.DeviceIdType.MESH,
        )

    def received_out(kind, peer):
        source, target, count = outs[kind]
        return pltpu.make_async_remote_copy(
            src_ref=source.at[token_rows(peer, count), :],
            dst_ref=target.at[:, head_columns(peer)],
            send_sem=out_send_sem.at[kind, peer],
            recv_sem=out_recv_sem.at[kind, peer],
            device_id={"seq": peer},
            device_id_type=pl.DeviceIdType.MESH,
        )

    def signal(semaphore, peer):
        pl.semaphore_signal(
            semaphore,
            inc=1,
            device_id={"seq": peer},
            device_id_type=pl.DeviceIdType.MESH,
        )

    def send(kinds, peers):
        for kind in kinds:
            for peer in peers:
                sent_in(kind, peer).start()

    barrier = pltpu.get_barrier_semaphore()
    near = [near_peer(step, 1) for step in range(1, half)]
    far = [far_peer(step, 1) for step in range(far_count)]
    for peer in far[:1] + near:
        signal(barrier, peer)
    pl.semaphore_wait(barrier, len(far[:1] + near))
    for peer in near:
        signal(far_in_sem, peer)
    for kinds, which in EARLY_ORDER:
        send(kinds, near if which == "near" else far[:1])
    if near:
        pl.semaphore_wait(far_in_sem, len(near))
    for kinds, which in LATE_ORDER:
        send(kinds, {"near": near, "rest": far[1:], "far": far}[which])

    gains = [
        pltpu.make_async_copy(source, target, gain_sem.at[index])
        for index, (source, target) in enumerate(
            (
                (video_query_gain_in, video_query_gain),
                (video_key_gain_in, video_key_gain),
                (audio_query_gain_in, audio_query_gain),
                (audio_key_gain_in, audio_key_gain),
            )
        )
    ]
    for gain in gains:
        gain.start()
    for kind in range(len(ins)):
        own_in(kind).start()

    ones = jnp.ones((arows * n, HEAD_DIM), jnp.bfloat16)
    av[:, HEAD_DIM:] = ones
    audio_self[:, HEAD_DIM:] = ones
    ones = jnp.ones((rows * n, HEAD_DIM), jnp.bfloat16)
    vv[:, HEAD_DIM:] = ones
    audio_sum[...] = jnp.zeros_like(audio_sum)

    def wait_kinds(kinds):
        for kind in kinds:
            own_in(kind).wait()

        def wait_peer(peer):
            for kind in kinds:
                received_in(kind, peer).wait_recv()

        over_peers(wait_peer, -1, False)

    def dot_t(left, right):
        return lax.dot_general(
            left, right, (((1,), (1,)), ((), ())), preferred_element_type=jnp.float32
        )

    def dot(left, right):
        return jnp.dot(left, right, preferred_element_type=jnp.float32)

    def self_attend(queries, key_rows, values):
        scores = dot_t(queries, key_rows)
        largest = jnp.max(scores, axis=1, keepdims=True)
        weights = jnp.exp2((scores - largest) * EXP2_SCALE).astype(jnp.bfloat16)
        both = dot(weights, values)
        return (both[:, :HEAD_DIM] / both[:, HEAD_DIM:]).astype(jnp.bfloat16)

    def unit(tokens):
        entries = tokens.astype(jnp.float32)
        mean = jnp.mean(entries * entries, axis=1, keepdims=True)
        return entries * lax.rsqrt(mean + 1e-06)

    own_head = pl.ds(me, 1)
    for gain in gains:
        gain.wait()
    wait_kinds((0, 1, 2))
    tokens = self_attend(aq[...], ak[...], av[...])
    audio_self[:, :HEAD_DIM] = tokens
    scaled = unit(tokens)
    audio_queries[...] = (scaled * audio_query_gain[own_head, :]).astype(jnp.bfloat16)
    audio_keys[...] = (scaled * audio_key_gain[own_head, :]).astype(jnp.bfloat16)

    wait_kinds((3, 4))

    def self_part(peers):
        here = [token_rows(peer, rows) for peer in peers]
        tokens = self_attend(jnp.concatenate([vq[one, :] for one in here], 0), vk[...], vv[...])
        scaled = unit(tokens)
        queries = (scaled * video_query_gain[own_head, :]).astype(jnp.bfloat16)
        key_rows = (scaled * video_key_gain[own_head, :]).astype(jnp.bfloat16)
        return tokens, queries, key_rows

    def audio_part(tokens, key_rows):
        weights = jnp.exp2(dot_t(audio_queries[...], key_rows) * EXP2_SCALE)
        values = jnp.concatenate([tokens, jnp.ones_like(tokens)], 1)
        audio_sum[...] += dot(weights.astype(jnp.bfloat16), values)

    def video_part(peers, tokens, queries):
        weights = jnp.exp2(dot_t(queries, audio_keys[...]) * EXP2_SCALE)
        both = dot(weights.astype(jnp.bfloat16), audio_self[...])
        cross = both[:, :HEAD_DIM] / both[:, HEAD_DIM:]
        mixed = (tokens.astype(jnp.float32) + cross).astype(jnp.bfloat16)
        for index, peer in enumerate(peers):
            video_mixed[token_rows(peer, rows), :] = mixed[index * rows : (index + 1) * rows]

    def send_audio(peer):
        sent_out(0, peer).start()

    others = [far_peer(step, -1) for step in range(far_count)]
    others += [near_peer(step, -1) for step in range(1, half)]
    group = GROUP if n % GROUP == 0 else 1
    for first in range(0, n, group):
        last = first + group == n
        here = others[first : first + group]
        for peer in here:
            received_in(5, peer).wait_recv()
        if last:
            own_in(5).wait()
        peers = here + [me] if last else here
        tokens, queries, key_rows = self_part(peers)
        if not last:
            video_part(peers, tokens, queries)
            for peer in here:
                sent_out(1, peer).start()
            audio_part(tokens, key_rows)
        else:
            audio_part(tokens, key_rows)
            both = audio_sum[...]
            cross = both[:, :HEAD_DIM] / both[:, HEAD_DIM:]
            audio_mixed[...] = (
                audio_self[:, :HEAD_DIM].astype(jnp.float32) + cross
            ).astype(jnp.bfloat16)
            own_out(0).start()
            over_peers(send_audio, 1, True)
            video_part(peers, tokens, queries)
            for peer in here:
                sent_out(1, peer).start()
            own_out(1).start()

    def finish_peer(peer):
        for kind in range(len(ins)):
            sent_in(kind, peer).wait_send()
        for kind in range(len(outs)):
            sent_out(kind, peer).wait_send()
            received_out(kind, peer).wait_recv()

    over_peers(finish_peer, 1, True)
    own_out(0).wait()
    own_out(1).wait()


def pass_on_kernel(video_in, audio_in, video_out, audio_out, sem):
    copies = (
        pltpu.make_async_copy(video_in, video_out, sem.at[0]),
        pltpu.make_async_copy(audio_in, audio_out, sem.at[1]),
    )
    for copy in copies:
        copy.start()
    for copy in copies:
        copy.wait()


GROUP = 2
KERNEL_BYTES = 24 * 2**20
EARLY_ORDER = (((0, 1, 2), "first"), ((0, 1, 2), "near"), ((3, 4), "first"), ((3, 4), "near"))
LATE_ORDER = (((0, 1, 2), "rest"), ((3, 4), "rest"), ((5,), "near"), ((5,), "far"))


def head_per_device(n, *arrays):
    video_q, audio_q = arrays[0], arrays[3]
    tokens, atokens = video_q.shape[0] * n, audio_q.shape[0] * n
    bf16, f32 = jnp.bfloat16, jnp.float32
    gains = [gain.reshape(n, HEAD_DIM) for gain in arrays[6:]]
    anywhere = pl.BlockSpec(memory_space=pl.ANY)
    operands = [
        pltpu.with_memory_space_constraint(one, pltpu.HBM) for one in (*arrays[:6], *gains)
    ]
    results = pl.pallas_call(
        functools.partial(attend_kernel, n),
        out_shape=(
            jax.ShapeDtypeStruct(video_q.shape, bf16),
            jax.ShapeDtypeStruct(audio_q.shape, bf16),
        ),
        in_specs=[anywhere] * 10,
        out_specs=(anywhere, anywhere),
        scratch_shapes=[
            pltpu.VMEM((tokens, HEAD_DIM), bf16),
            pltpu.VMEM((tokens, HEAD_DIM), bf16),
            pltpu.VMEM((tokens, 2 * HEAD_DIM), bf16),
            pltpu.VMEM((atokens, HEAD_DIM), bf16),
            pltpu.VMEM((atokens, HEAD_DIM), bf16),
            pltpu.VMEM((atokens, 2 * HEAD_DIM), bf16),
            pltpu.VMEM((atokens, 2 * HEAD_DIM), bf16),
            pltpu.VMEM((atokens, HEAD_DIM), bf16),
            pltpu.VMEM((atokens, HEAD_DIM), bf16),
            pltpu.VMEM((atokens, 2 * HEAD_DIM), f32),
            pltpu.VMEM((tokens, HEAD_DIM), bf16),
            pltpu.VMEM((atokens, HEAD_DIM), bf16),
            pltpu.SemaphoreType.DMA((6, n)),
            pltpu.SemaphoreType.DMA((6, n)),
            pltpu.SemaphoreType.DMA((6,)),
            pltpu.SemaphoreType.DMA((2, n)),
            pltpu.SemaphoreType.DMA((2, n)),
            pltpu.SemaphoreType.DMA((2,)),
            pltpu.SemaphoreType.REGULAR,
            *[pltpu.VMEM((n, HEAD_DIM), f32)] * 4,
            pltpu.SemaphoreType.DMA((4,)),
        ],
        compiler_params=pltpu.CompilerParams(
            collective_id=0, has_side_effects=True, vmem_limit_bytes=KERNEL_BYTES
        ),
    )(*operands)
    return pl.pallas_call(
        pass_on_kernel,
        out_shape=(
            jax.ShapeDtypeStruct(video_q.shape, bf16),
            jax.ShapeDtypeStruct(audio_q.shape, bf16),
        ),
        in_specs=[anywhere] * 2,
        out_specs=(anywhere, anywhere),
        scratch_shapes=[pltpu.SemaphoreType.DMA((2,))],
        compiler_params=pltpu.CompilerParams(vmem_limit_bytes=KERNEL_BYTES // 4),
    )(*results)


def solution(mesh):
    in_specs = (
        P(("clips", "seq"), "head"),
        P(("clips", "seq"), "head"),
        P(("clips", "seq"), "head"),
        P(("clips", "seq"), "head"),
        P(("clips", "seq"), "head"),
        P(("clips", "seq"), "head"),
        P("head"),
        P("head"),
        P("head"),
        P("head"),
    )
    out_specs = (P(("clips", "seq"), "head"), P(("clips", "seq"), "head"))
    sizes = dict(mesh.shape)

    def body(*arrays):
        video_q, audio_q = arrays[0], arrays[3]
        if (
            video_q.shape[1] == sizes["seq"] * HEAD_DIM
            and video_q.shape[0] % 16 == 0
            and audio_q.shape[0] % 16 == 0
        ):
            return head_per_device(sizes["seq"], *arrays)
        return per_device(*arrays)

    return jax.shard_map(
        body, mesh=mesh, in_specs=in_specs, out_specs=out_specs, check_vma=False
    )
```
